32 devices in a mesh: lat: 4 (over y, x), lon: 8 (over z, core).
Axes of the slice: x: 2, y: 2, z: 4, core: 2. Of those that a mesh axis runs over, the one named last changes fastest.
Arguments:
- adjoint_in: float32 [4, 79, 32, 1024], P(None, None, 'lat', 'lon'), may hold values from -6 to 6
- fractions: bfloat16 [4, 4, 79, 32, 1024], P(None, None, None, 'lat', 'lon'), may hold values from 0 to 0.95, as said below
- profiles: bfloat16 [2, 79, 32, 1024], P(None, None, 'lat', 'lon'), may hold values from 0.099609375 to 1
- kernel: bfloat16 [79, 79], replicated, may hold values from -0.625 to 0.625
- obs_weights: bfloat16 [79, 32768], P(None, ('lat', 'lon')), may hold values from 0.099609375 to 1.5
- obs_resid: bfloat16 [4, 32768], P(None, ('lat', 'lon')), may hold values from -5 to 5
- obs_cols: int32 [32768], P(('lat', 'lon')), may hold values from 0 to 1023
- obs_owner: int32 [4096, 1], P(('lat', 'lon')), may hold values from 0 to 31; in each aligned block of 128 rows (0 to 127, 128 to 255, ...) at most 6 rows name the same one
- obs_count: int32 [4096], P(('lat', 'lon')), may hold values from 5 to 8
- lat_matrix: bfloat16 [32, 32], replicated, as said below
- lon_matrix: bfloat16 [1024, 1024], P('lon'), as said below
Outputs:
- adjoint_out: float32 [4, 79, 32, 1024], P(None, None, 'lat', 'lon')
- smoothed_gradient: float32 [4, 32, 1024], P(None, 'lat', 'lon')
The draws below stay inside these ranges and needn't reach their ends.
Inputs may be any that keep to these rules, and one draw needn't show every extreme that they name: `fractions`: fractions are nonnegative and the four of one cell and step sum to at most 0.95. `obs_owner`: owners are numbered as lat index times 8 plus lon index. Among the blocks of one device at most 6 share an owner. `obs_cols`: A tile's columns are numbered row by row: row within the tile times 128 plus column within the tile. The first obs_count slots of a block are valid, the others are padding. `lat_matrix`: Symmetric. `lon_matrix`: Symmetric.
All inputs are finite; a program needn't handle non-finite values.
Results may differ from the reference program's by a relative error of at most 0.0041.
Values may be sent and summed in bfloat16 or wider, within the bound.
No kernel may reach another device: no remote copies, remote signals or barrier semaphores. Data moves between devices by JAX's collectives and lax.ppermute only.
A program may use at most 192 MiB of HBM per device.

```python
import math
import jax
import jax.numpy as jnp
import numpy as np
from jax import lax

TRACERS = 4
LEV = 79
STEPS = 4
SLOTS = 8
CAPACITY = 6
LAT_DEV = 8
LON_DEV = 128
BLK_DEV = 128
NLAT = 32
NLON = 1024
CELLS_DEV = 1024
NBLK = 4096
NSND = 32768
N_LON = 8
DEVICES = 32


def symmetric_matrix(key, matrix_order):
    key_one, key_two = jax.random.split(key)
    noise_part = jax.random.normal(key_one, (matrix_order, matrix_order), jnp.float32)
    diagonal = jax.random.uniform(key_two, (matrix_order,), jnp.float32, 1.0, 2.0)
    scaled = (noise_part + noise_part.T) * (0.3 / math.sqrt(matrix_order))
    return (jnp.diag(diagonal) + scaled).astype(jnp.bfloat16)


def draw_fractions(key, part):
    key_one, key_two = jax.random.split(jax.random.fold_in(key, 5))
    shares = jax.random.uniform(key_one, (STEPS, 4, LEV, NLAT, NLON), jnp.float32, 0.05, 1.0)
    totals = jax.random.uniform(key_two, (STEPS, 1, LEV, NLAT, NLON), jnp.float32, 0.3, 0.95)
    return (totals * shares / jnp.sum(shares, axis=1, keepdims=True)).astype(jnp.bfloat16)


def draw_lat_matrix(key, part):
    return symmetric_matrix(jax.random.fold_in(key, 11), NLAT)


def draw_lon_matrix(key, part):
    return symmetric_matrix(jax.random.fold_in(key, 23), NLON)


def plant(entries, rng, low, largest):
    longest = entries.shape.index(max(entries.shape))
    spots = []
    for shift in (0, 1):
        where = [jax.random.randint(jax.random.fold_in(rng, axis), (), 0, length) for axis, length in enumerate(entries.shape)]
        where[longest] = (where[longest] + shift) % entries.shape[longest]
        spots.append(tuple(where))
    return entries.at[spots[0]].set(low).at[spots[1]].set(largest)


def block_levels(own_key, dims, cuts, low, top_value):
    loudness, own = 1.0, jax.random.fold_in(own_key, 6)
    for position, shards_of in cuts:
        heights = jnp.exp(jax.random.uniform(jax.random.fold_in(own, position), (shards_of,), jnp.float32, low / len(cuts), top_value / len(cuts)))
        loudness = loudness * jnp.repeat(heights, dims[position] // shards_of).reshape([-1 if axis == position else 1 for axis in range(len(dims))])
    return loudness


def routed_block(rng, own, number, rows, count, top, reach, slope):
    ranking = jax.random.permutation(rng, count)
    heavy_load, common = load_shares(count, rows * top, reach, slope, True), load_shares(count, rows * top, reach, slope, False)
    places = jnp.arange(count)

    def named(lengths, turn):
        used = int((lengths > 0).sum())
        fixed = max(1, used // 4)
        passed = fixed + (places - fixed + turn * (used - fixed)) % max(1, count - fixed)
        return jnp.zeros((count,), jnp.int32).at[ranking[jnp.where(places < fixed, places, passed)]].set(jnp.asarray(lengths, jnp.int32))

    lengths = jnp.where(number % 4 == 0, named(heavy_load, number // 4), named(common, number - number // 4 - 1))
    mixed = jax.random.permutation(jax.random.fold_in(own, 3), count)
    donor, taker = mixed[0:count // 2 * 2:2], mixed[1:count // 2 * 2:2]
    margin = jnp.minimum(lengths[donor] - 1, reach - lengths[taker]) // 2
    margin = jnp.where((donor == ranking[0]) | (taker == ranking[0]) | (lengths[taker] == 0), 0, jnp.maximum(margin, 0))
    passed = jax.random.randint(jax.random.fold_in(own, 4), (count // 2,), 0, 1 << 20) % (margin + 1)
    lengths = lengths.at[donor].add(-passed).at[taker].add(passed)
    items = jnp.searchsorted(jnp.cumsum(lengths), jnp.arange(rows * top), side="right").astype(jnp.int32)
    grid = items.reshape(top, rows).T
    grid = grid[jax.random.permutation(jax.random.fold_in(own, 1), rows)]
    turn = jax.random.randint(jax.random.fold_in(own, 2), (rows, 1), 0, top)
    return jnp.take_along_axis(grid, (jnp.arange(top)[None, :] + turn) % top, axis=1)


def load_shares(count, total, reach, skew, full):
    loads = [(1 << 20) // math.isqrt(rank ** skew) + 1 for rank in range(1, count + 1)]
    largest = reach if full else min(reach, max(-(-total // count), total * loads[0] // sum(loads)))
    least = 1 if total - largest >= count - 1 else 0
    holding, surplus = [largest] + [least] * (count - 1), total - largest - least * (count - 1)
    while surplus > 0:
        movable = [i for i in range(1, count) if holding[i] < largest] or [i for i in range(1, count) if holding[i] < reach]
        whole, remaining = sum([loads[i] for i in movable]), surplus
        for i in movable:
            extra = min(reach - holding[i], max(1, remaining * loads[i] // whole), surplus)
            holding[i] = holding[i] + extra
            surplus = surplus - extra
    return np.array(holding)


def centred(rng, extent, width, most, cuts=(), dtype=jnp.bfloat16):
    factor_of = block_levels(rng, extent, cuts, -0.22, 0.18) if cuts else 1.0
    values = jax.random.normal(rng, extent, jnp.float32) * width * factor_of
    return jnp.minimum(jnp.maximum(values, -most), most).astype(dtype)


def setup_inputs(seed: int = 0) -> dict:
    seeds = jax.random.split(jax.random.key(seed), 12)
    adjoint_in = centred(seeds[0], (TRACERS, LEV, NLAT, NLON), 1.0, 6.0, ((2, 4), (3, 8)), jnp.float32)
    fractions = draw_fractions(jax.random.fold_in(seeds[11], 71), 0)
    profiles = jnp.clip(jnp.exp(math.log(1.0) - 2.306499 * jax.random.uniform(seeds[2], (2, LEV, NLAT, NLON), jnp.float32) ** block_levels(seeds[2], (2, LEV, NLAT, NLON), ((2, 4), (3, 8)), -0.2, 0.2)), 0.099609375, 1.0).astype(jnp.bfloat16)
    kernel = centred(seeds[3], (LEV, LEV), LEV ** -0.5, 0.625)
    obs_weights = jnp.clip(0.099609375 + 1.4003906 * jax.random.uniform(seeds[4], (LEV, NSND), jnp.float32) ** block_levels(seeds[4], (LEV, NSND), ((1, 32),), -0.2, 0.2), 0.099609375, 1.5).astype(jnp.bfloat16)
    obs_resid = centred(seeds[5], (TRACERS, NSND), 1.0, 5.0, ((1, 32),))
    obs_cols = plant(jax.random.randint(seeds[6], (NSND,), 0, CELLS_DEV), jax.random.fold_in(seeds[6], 1), 0, CELLS_DEV - 1).astype(jnp.int32)
    obs_owner_keys = jax.random.split(jax.random.fold_in(seeds[7], 1), NBLK // BLK_DEV)
    obs_owner_turns = jax.random.permutation(jax.random.fold_in(seeds[7], 3), NBLK // BLK_DEV)
    obs_owner = jax.vmap(lambda own, number: routed_block(jax.random.fold_in(seeds[7], 2), own, number, BLK_DEV, DEVICES, 1, CAPACITY, 2))(obs_owner_keys, obs_owner_turns).reshape((NBLK, 1))
    obs_count = plant(jax.random.randint(seeds[8], (NBLK,), 5, SLOTS + 1), jax.random.fold_in(seeds[8], 1), 5, SLOTS).astype(jnp.int32)
    lat_matrix = draw_lat_matrix(jax.random.fold_in(seeds[11], 71), 0)
    lon_matrix = draw_lon_matrix(jax.random.fold_in(seeds[11], 71), 0)
    return dict(adjoint_in=adjoint_in, fractions=fractions, profiles=profiles, kernel=kernel, obs_weights=obs_weights, obs_resid=obs_resid, obs_cols=obs_cols, obs_owner=obs_owner, obs_count=obs_count, lat_matrix=lat_matrix, lon_matrix=lon_matrix)


def convect(adjoint, kernel, entrain, detrain):
    lowered = (detrain * adjoint).astype(jnp.bfloat16)
    mixing = jnp.einsum("kj,tkyx->tjyx", kernel.astype(jnp.float32), lowered.astype(jnp.float32), precision=lax.Precision.HIGHEST)
    return adjoint + entrain * mixing


def transport(field_in, fraction):
    east_side = jnp.roll(field_in, -1, axis=3)
    west_side = jnp.roll(field_in, 1, axis=3)
    padded = jnp.pad(field_in, ((0, 0), (0, 0), (1, 1), (0, 0)))
    north_side = padded[:, :, 2:, :]
    south_side = padded[:, :, :-2, :]
    remain = 1.0 - fraction[0] - fraction[1] - fraction[2] - fraction[3]
    return (remain * field_in + fraction[0] * east_side + fraction[1] * west_side
            + fraction[2] * north_side + fraction[3] * south_side)


def sounding_forcing(obs_weights, obs_resid, obs_cols, obs_owner, obs_count):
    blocks = obs_count.shape[0]
    slot_index = jnp.tile(jnp.arange(SLOTS).astype(jnp.int32), blocks)
    owner_device = jnp.repeat(obs_owner[:, 0], SLOTS).astype(jnp.int32)
    live_count = jnp.repeat(obs_count, SLOTS).astype(jnp.int32)
    row_index = (owner_device // N_LON) * LAT_DEV + obs_cols // LON_DEV
    col_index = (owner_device % N_LON) * LON_DEV + obs_cols % LON_DEV
    cell_index = jnp.where(slot_index < live_count, row_index * NLON + col_index, NLAT * NLON).astype(jnp.int32)
    contrib = obs_weights.astype(jnp.float32)[None, :, :] * obs_resid.astype(jnp.float32)[:, None, :]
    flattened = jnp.zeros((TRACERS, LEV, NLAT * NLON), jnp.float32)
    flattened = flattened.at[:, :, cell_index].add(contrib, mode="drop")
    return flattened.reshape(TRACERS, LEV, NLAT, NLON)


def reference(adjoint_in, fractions, profiles, kernel, obs_weights, obs_resid, obs_cols, obs_owner, obs_count, lat_matrix, lon_matrix):
    entrain = profiles[0].astype(jnp.float32)
    detrain = profiles[1].astype(jnp.float32)
    forcing = sounding_forcing(obs_weights, obs_resid, obs_cols, obs_owner, obs_count)
    adjoint = adjoint_in
    surface = jnp.zeros((TRACERS, NLAT, NLON), jnp.float32)
    for step_index in range(STEPS - 1, -1, -1):
        fraction = fractions[step_index].astype(jnp.float32)
        adjoint = transport(convect(adjoint, kernel, entrain, detrain), fraction)
        if step_index == 0:
            adjoint = adjoint + forcing
        surface = surface + adjoint[:, 0]
    surface_low = surface.astype(jnp.bfloat16)
    lon_smoothed = jnp.einsum("tyx,xj->tyj", surface_low.astype(jnp.float32), lon_matrix.astype(jnp.float32), precision=lax.Precision.HIGHEST).astype(jnp.bfloat16)
    smoothed_gradient = jnp.einsum("iy,tyj->tij", lat_matrix.astype(jnp.float32), lon_smoothed.astype(jnp.float32), precision=lax.Precision.HIGHEST)
    return adjoint, smoothed_gradient
```

```python
import functools

import jax
import jax.numpy as jnp
from jax import lax
from jax.experimental import pallas as pl
from jax.experimental.pallas import tpu as pltpu
from jax.sharding import PartitionSpec as P

STEPS = 4
CAPACITY = 6
F32 = jnp.float32
BF16 = jnp.bfloat16
BOTH = ("lat", "lon")
LANES = 128


def iota(shape, dim):
    return lax.broadcasted_iota(jnp.int32, shape, dim)


def dot_nt(a, b):
    return lax.dot_general(a, b, (((1,), (1,)), ((), ())), preferred_element_type=F32)


def dot_tn(a, b):
    return lax.dot_general(a, b, (((0,), (0,)), ((), ())), preferred_element_type=F32)


def full(shape):
    return pl.BlockSpec(shape, lambda i: (0,) * len(shape))


def params(limit=48 << 20):
    return pltpu.CompilerParams(vmem_limit_bytes=limit)


def expand_kernel(kernel, levels, padded, rows):
    size = padded * rows
    spread = (iota((size, levels), 0) // rows == iota((size, levels), 1)).astype(BF16)
    half = dot_nt(spread, kernel).astype(BF16)
    whole = dot_nt(half, spread)
    same = iota((size, size), 0) % rows == iota((size, size), 1) % rows
    return jnp.where(same, whole, 0.0).astype(BF16)


def convect(dims, adj, low, mix, kron, profiles, mixed):
    tracers, levels, rows = dims
    mix[...] = jnp.dot(kron[...], low[...], preferred_element_type=F32)

    def body(k, carry):
        entrain = profiles[0, k].astype(F32)
        start = pl.multiple_of(k * rows, rows)
        for t in range(tracers):
            at = pl.multiple_of((t * levels + k) * rows, rows)
            mixed[pl.ds(at, rows), :] = adj[pl.ds(at, rows), :] + entrain * mix[
                pl.ds(start, rows), t * LANES : (t + 1) * LANES
            ]
        return carry

    lax.fori_loop(0, levels, body, 0)


def send_edges(dims, mixed, up, down, west, east):
    tracers, levels, rows = dims
    count = tracers * levels
    lat = lax.axis_index("lat")
    last = lax.axis_size("lat") - 1
    first_row = mixed[pl.ds(0, count, stride=rows), :]
    last_row = mixed[pl.ds(rows - 1, count, stride=rows), :]
    up[...] = jnp.where(lat < last, last_row, 0.0).astype(BF16)
    down[...] = jnp.where(lat > 0, first_row, 0.0).astype(BF16)
    lane = iota((rows, LANES), 1)
    sub = iota((rows, LANES), 0)
    pick = ((sub == 0) & (lane == 0)) | ((sub == 1) & (lane == LANES - 1))
    sides = dot_nt(pick.astype(BF16), mixed[...].astype(BF16))
    west[...] = sides[0:1]
    east[...] = sides[1:2]


def store_low(low, k2, rows, t, parts):
    low[pl.ds(pl.multiple_of(k2 * 2 * rows, 2 * rows), 2 * rows), t * LANES : (t + 1) * LANES] = jnp.concatenate(
        parts, axis=0
    ).astype(BF16)


def over_levels(levels, body):
    def pair(k2, carry):
        body(k2, (2 * k2, 2 * k2 + 1))
        return carry

    lax.fori_loop(0, levels // 2, pair, 0)
    if levels % 2:
        body(levels // 2, (levels - 1,))


def first_body(dims, kernel, profiles, adjoint, mixed, kron, up, down, west, east, low, mix):
    tracers, levels, rows = dims
    kron[...] = expand_kernel(kernel[...], levels, low.shape[0] // rows, rows)

    def body(k2, ks):
        detrains = [profiles[1, k].astype(F32) for k in ks]
        for t in range(tracers):
            parts = [
                d * adjoint[pl.ds(pl.multiple_of((t * levels + k) * rows, rows), rows), :] for d, k in zip(detrains, ks)
            ]
            store_low(low, k2, rows, t, parts if len(parts) == 2 else parts + [jnp.zeros_like(parts[0])])

    over_levels(levels, body)
    convect(dims, adjoint, low, mix, kron, profiles, mixed)
    send_edges(dims, mixed, up, down, west, east)


def unpack_halo(dims, north, south, east, west, north_scr, south_scr, sides):
    tracers, levels, rows = dims
    count = tracers * levels
    north_scr[0:count, :] = north[...].astype(F32)
    south_scr[0:count, :] = south[...].astype(F32)
    sub = iota((rows, count * rows), 0)
    got = jnp.where(sub == 0, east[...], jnp.where(sub == 1, west[...], 0.0)).astype(BF16)
    lane = iota((rows, LANES), 1)
    sub = iota((rows, LANES), 0)
    place = (((sub == 0) & (lane == LANES - 1)) | ((sub == 1) & (lane == 0))).astype(BF16)
    sides[...] = dot_tn(got, place)


def transport(dims, k, fraction, mixed, north_scr, south_scr, sides):
    tracers, levels, rows = dims
    f = [fraction[0, d, k].astype(F32) for d in range(4)]
    remain = 1.0 - f[0] - f[1] - f[2] - f[3]
    lane = iota((rows, LANES), 1)
    sub = iota((rows, LANES), 0)
    out = []
    for t in range(tracers):
        index = t * levels + k
        at = pl.ds(pl.multiple_of(index * rows, rows), rows)
        m = mixed[at, :]
        side = sides[at, :]
        east = jnp.where(lane == LANES - 1, side, pltpu.roll(m, LANES - 1, 1))
        west = jnp.where(lane == 0, side, pltpu.roll(m, 1, 1))
        north = jnp.where(
            sub == rows - 1,
            jnp.broadcast_to(north_scr[pl.ds(index, 1), :], (rows, LANES)),
            pltpu.roll(m, rows - 1, 0),
        )
        south = jnp.where(
            sub == 0, jnp.broadcast_to(south_scr[pl.ds(index, 1), :], (rows, LANES)), pltpu.roll(m, 1, 0)
        )
        out.append((at, remain * m + f[0] * east + f[1] * west + f[2] * north + f[3] * south))
    return out


def step_body(dims, mixed, north, south, east, west, fraction, profiles, kron, surface, *rest):
    new_mixed, up, down, to_west, to_east, new_surface, north_scr, south_scr, sides, adj, low, mix = rest
    tracers, levels, rows = dims
    unpack_halo(dims, north, south, east, west, north_scr, south_scr, sides)

    def body(k2, ks):
        parts = [[] for _ in range(tracers)]
        for k in ks:
            detrain = profiles[1, k].astype(F32)
            for t, (at, value) in enumerate(transport(dims, k, fraction, mixed, north_scr, south_scr, sides)):
                adj[at, :] = value
                parts[t].append(detrain * value)
        for t in range(tracers):
            two = parts[t] if len(ks) == 2 else parts[t] + [jnp.zeros_like(parts[t][0])]
            store_low(low, k2, rows, t, two)

    over_levels(levels, body)
    convect(dims, adj, low, mix, kron, profiles, new_mixed)
    send_edges(dims, new_mixed, up, down, to_west, to_east)
    for t in range(tracers):
        at = t * levels * rows
        new_surface[t * rows : (t + 1) * rows, :] = surface[t * rows : (t + 1) * rows, :] + adj[at : at + rows, :]


def last_body(dims, mixed, north, south, east, west, fraction, forcing, surface, *rest):
    adjoint, surface_low, north_scr, south_scr, sides = rest
    tracers, levels, rows = dims
    unpack_halo(dims, north, south, east, west, north_scr, south_scr, sides)

    def body(k, carry):
        start = pl.multiple_of(k * rows, rows)
        for t, (at, value) in enumerate(transport(dims, k, fraction, mixed, north_scr, south_scr, sides)):
            adjoint[at, :] = value + forcing[pl.ds(start, rows), t * LANES : (t + 1) * LANES]
        return carry

    lax.fori_loop(0, levels, body, 0)
    for t in range(tracers):
        at = t * levels * rows
        total = surface[t * rows : (t + 1) * rows, :] + adjoint[at : at + rows, :]
        surface_low[t * rows : (t + 1) * rows, :] = total.astype(BF16)


def pack_body(sizes, owner, count, cols, weights, resid, out):
    devices, blocks, slots, levels, tracers, chunk = sizes
    own = owner[...].astype(F32)
    wide = jnp.broadcast_to(own, (blocks, blocks))
    below = iota((blocks, blocks), 0)
    along = iota((blocks, blocks), 1)
    own_col = jnp.sum(jnp.where(below == along, wide, 0.0), axis=1, keepdims=True)
    earlier = jnp.where((own_col == wide) & (below < along), 1.0, 0.0)
    rank = jnp.sum(earlier, axis=0, keepdims=True)
    table = jnp.concatenate(
        [own, rank, count[...].astype(F32), jnp.zeros((5, blocks), F32)], axis=0
    ).astype(BF16)
    total = blocks * slots
    spread = (iota((blocks, total), 1) // slots == iota((blocks, total), 0)).astype(BF16)
    each = jnp.dot(table, spread, preferred_element_type=F32)
    slot = iota((1, total), 1) % slots
    target = (each[0:1].astype(jnp.int32) * CAPACITY + each[1:2].astype(jnp.int32)) * slots + slot
    valid = slot < each[2:3].astype(jnp.int32)
    held = jnp.where(valid, resid[...].astype(F32), 0.0)
    place = cols[...]
    high = (place // LANES).astype(F32)
    lower = (place % LANES).astype(F32)
    fill = LANES - levels - tracers - 2
    data = jnp.concatenate(
        [weights[...].astype(F32), held, high, lower, jnp.zeros((fill, total), F32)], axis=0
    ).astype(BF16)

    def body(c, carry):
        at = pl.multiple_of(c * chunk, chunk)
        pick = jnp.where(iota((chunk, total), 0) + at == target, 1.0, 0.0).astype(BF16)
        out[pl.ds(at, chunk), :] = dot_nt(pick, data).astype(BF16)
        return carry

    lax.fori_loop(0, out.shape[0] // chunk, body, 0)


def forcing_body(dims, chunk, got, forcing, left, right):
    tracers, levels, rows = dims
    padded = left.shape[0] // rows

    def body(c, carry):
        at = pl.multiple_of(c * chunk, chunk)
        part = got[pl.ds(at, chunk), :].astype(F32)
        lane = iota((chunk, LANES), 1).astype(F32)
        hit = part[:, levels + tracers + 1 : levels + tracers + 2] == lane
        for t in range(tracers):
            right[:, t * LANES : (t + 1) * LANES] = jnp.where(
                hit, part[:, levels + t : levels + t + 1], 0.0
            ).astype(BF16)
        turned = part.T
        high = turned[levels + tracers : levels + tracers + 1, :]
        sub = iota((rows, chunk), 0).astype(F32)
        mine = sub == high
        for k2 in range(padded // 2):
            two = []
            for k in (2 * k2, 2 * k2 + 1):
                two.append(jnp.where(mine, turned[k : k + 1, :], 0.0) if k < levels else jnp.zeros((rows, chunk), F32))
            left[2 * k2 * rows : (2 * k2 + 2) * rows, :] = jnp.concatenate(two, axis=0).astype(BF16)
        value = jnp.dot(left[...], right[...], preferred_element_type=F32)

        @pl.when(c == 0)
        def _():
            forcing[...] = value

        @pl.when(c > 0)
        def _():
            forcing[...] += value

        return carry

    lax.fori_loop(0, got.shape[0] // chunk, body, 0)


def lon_body(got, matrix, out):
    count = got.shape[0]
    total = jnp.zeros(out.shape, F32)
    for z in range(count):
        total = total + dot_nt(got[z], matrix[:, z * LANES : (z + 1) * LANES])
    out[...] = total.astype(BF16)


def lat_body(tracers, rows, got, matrix, out):
    bands = got.shape[0]
    size = tracers * rows
    lat = lax.axis_index("lat")
    own = matrix[pl.ds(pl.multiple_of(lat * rows, rows), rows), :]
    own = jnp.concatenate([own] * tracers, axis=0)
    total = jnp.zeros(out.shape, F32)
    for b in range(bands):
        block = own[:, b * rows : (b + 1) * rows]
        block = jnp.concatenate([block] * tracers, axis=1)
        same = iota((size, size), 0) // rows == iota((size, size), 1) // rows
        total = total + jnp.dot(
            jnp.where(same, block, 0.0).astype(BF16), got[b], preferred_element_type=F32
        )
    out[...] = total


def ring(axis, step):
    count = lax.axis_size(axis)
    return [(i, (i + step) % count) for i in range(count)]


def exchange(up, down, to_west, to_east):
    south = lax.ppermute(up, "lat", ring("lat", 1))
    north = lax.ppermute(down, "lat", ring("lat", -1))
    east = lax.ppermute(to_west, "lon", ring("lon", -1))
    west = lax.ppermute(to_east, "lon", ring("lon", 1))
    return north, south, east, west


def shards(
    adjoint_in,
    fractions,
    profiles,
    kernel,
    obs_weights,
    obs_resid,
    obs_cols,
    obs_owner,
    obs_count,
    lat_matrix,
    lon_matrix,
):
    dims = tracers, levels, rows = adjoint_in.shape[:3]
    assert adjoint_in.shape[3] == LANES
    padded = (levels + 1) // 2 * 2
    count = tracers * levels
    cells = count * rows
    wide = tracers * LANES
    devices = lax.axis_size(BOTH)
    state = jax.ShapeDtypeStruct((cells, LANES), F32)
    row_edge = jax.ShapeDtypeStruct((count, LANES), BF16)
    side_edge = jax.ShapeDtypeStruct((1, cells), F32)
    edges = [row_edge, row_edge, side_edge, side_edge]
    kron_type = jax.ShapeDtypeStruct((padded * rows, padded * rows), BF16)
    surface_type = jax.ShapeDtypeStruct((tracers * rows, LANES), F32)
    low_scr = pltpu.VMEM((padded * rows, wide), BF16)
    mix_scr = pltpu.VMEM((padded * rows, wide), F32)
    halo_scr = [
        pltpu.VMEM(((count + 7) // 8 * 8, LANES), F32),
        pltpu.VMEM(((count + 7) // 8 * 8, LANES), F32),
        pltpu.VMEM((cells, LANES), F32),
    ]

    def spec(leaf):
        return full(leaf.shape)

    mixed, kron, *out = pl.pallas_call(
        functools.partial(first_body, dims),
        grid=(1,),
        out_shape=[state, kron_type] + edges,
        in_specs=[full(kernel.shape), full(profiles.shape), spec(state)],
        out_specs=[spec(s) for s in [state, kron_type] + edges],
        scratch_shapes=[low_scr, mix_scr],
        compiler_params=params(),
        name="first",
    )(kernel, profiles, adjoint_in.reshape(cells, LANES))
    halo = exchange(*out)

    blocks = obs_count.shape[0]
    slots = obs_cols.shape[0] // blocks
    rows_out = devices * CAPACITY * slots
    packed = pl.pallas_call(
        functools.partial(pack_body, (devices, blocks, slots, levels, tracers, 8 * CAPACITY * slots)),
        out_shape=jax.ShapeDtypeStruct((rows_out, LANES), BF16),
        compiler_params=params(),
        name="pack",
    )(
        obs_owner.reshape(1, blocks),
        obs_count.reshape(1, blocks),
        obs_cols.reshape(1, blocks * slots),
        obs_weights,
        obs_resid,
    )
    got = lax.all_to_all(
        packed.reshape(devices, CAPACITY * slots, LANES), BOTH, split_axis=0, concat_axis=0, tiled=True
    )
    chunk = min(rows_out, 1536)
    forcing = pl.pallas_call(
        functools.partial(forcing_body, dims, chunk),
        out_shape=jax.ShapeDtypeStruct((padded * rows, wide), F32),
        scratch_shapes=[pltpu.VMEM((padded * rows, chunk), BF16), pltpu.VMEM((chunk, wide), BF16)],
        compiler_params=params(),
        name="forcing",
    )(got.reshape(rows_out, LANES))

    surface = jnp.zeros(surface_type.shape, F32)
    for step_index in range(STEPS - 1, 0, -1):
        frac_spec = pl.BlockSpec((1,) + fractions.shape[1:], lambda i, n=step_index: (n, 0, 0, 0, 0))
        mixed, *out, surface = pl.pallas_call(
            functools.partial(step_body, dims),
            grid=(1,),
            out_shape=[state] + edges + [surface_type],
            in_specs=[spec(state), spec(row_edge), spec(row_edge), spec(side_edge), spec(side_edge)]
            + [frac_spec, full(profiles.shape), spec(kron_type), spec(surface_type)],
            out_specs=[spec(s) for s in [state] + edges + [surface_type]],
            scratch_shapes=halo_scr + [pltpu.VMEM((cells, LANES), F32), low_scr, mix_scr],
            compiler_params=params(),
            name="step",
        )(mixed, *halo, fractions, profiles, kron, surface)
        halo = exchange(*out)

    frac_spec = pl.BlockSpec((1,) + fractions.shape[1:], lambda i: (0, 0, 0, 0, 0))
    low_type = jax.ShapeDtypeStruct(surface_type.shape, BF16)
    adjoint, surface_low = pl.pallas_call(
        functools.partial(last_body, dims),
        grid=(1,),
        out_shape=[state, low_type],
        in_specs=[spec(state), spec(row_edge), spec(row_edge), spec(side_edge), spec(side_edge)]
        + [frac_spec, full(forcing.shape), spec(surface_type)],
        out_specs=[spec(state), spec(low_type)],
        scratch_shapes=halo_scr,
        compiler_params=params(),
        name="last",
    )(mixed, *halo, fractions, forcing, surface)

    lon_count = lax.axis_size("lon")
    spread = jnp.broadcast_to(surface_low[None], (lon_count,) + surface_low.shape)
    band = lax.all_to_all(spread, "lon", split_axis=0, concat_axis=0, tiled=True)
    across = pl.pallas_call(
        lon_body,
        out_shape=low_type,
        compiler_params=params(),
        name="lon_smooth",
    )(band, lon_matrix)
    column = lax.all_gather(across, "lat", axis=0)
    smoothed = pl.pallas_call(
        functools.partial(lat_body, tracers, rows),
        out_shape=surface_type,
        compiler_params=params(),
        name="lat_smooth",
    )(column, lat_matrix)
    return adjoint.reshape(adjoint_in.shape), smoothed.reshape(tracers, rows, LANES)


def solution(mesh):
    placed = (
        P(None, None, "lat", "lon"),
        P(None, None, None, "lat", "lon"),
        P(None, None, "lat", "lon"),
        P(),
        P(None, BOTH),
        P(None, BOTH),
        P(BOTH),
        P(BOTH, None),
        P(BOTH),
        P(),
        P("lon", None),
    )
    return jax.shard_map(
        shards,
        mesh=mesh,
        in_specs=placed,
        out_specs=(P(None, None, "lat", "lon"), P(None, "lat", "lon")),
        check_vma=False,
    )
```

```python
import functools

import jax
import jax.numpy as jnp
from jax import lax
from jax.experimental import pallas as pl
from jax.experimental.pallas import tpu as pltpu
from jax.sharding import PartitionSpec as P

STEPS = 4
CAPACITY = 6
F32 = jnp.float32
BF16 = jnp.bfloat16
BOTH = ("lat", "lon")
LANES = 128


def aligned(value, by):
    return value if isinstance(value, int) else pl.multiple_of(value, by)


def iota(shape, dim):
    return lax.broadcasted_iota(jnp.int32, shape, dim)


def dot_nt(a, b):
    return lax.dot_general(a, b, (((1,), (1,)), ((), ())), preferred_element_type=F32)


def dot_tn(a, b):
    return lax.dot_general(a, b, (((0,), (0,)), ((), ())), preferred_element_type=F32)


def full(shape):
    return pl.BlockSpec(shape, lambda i: (0,) * len(shape))


def params(limit=48 << 20):
    return pltpu.CompilerParams(vmem_limit_bytes=limit)


def expand_kernel(kernel, levels, padded, rows):
    size = padded * rows
    spread = (iota((size, levels), 0) // rows == iota((size, levels), 1)).astype(BF16)
    half = dot_nt(spread, kernel).astype(BF16)
    whole = dot_nt(half, spread)
    same = iota((size, size), 0) % rows == iota((size, size), 1) % rows
    return jnp.where(same, whole, 0.0).astype(BF16)


def convect(dims, adj, low, mix, kron, profiles, mixed):
    tracers, levels, rows = dims
    mix[...] = jnp.dot(kron[...], low[...], preferred_element_type=F32)

    def body(k2, ks):
        for k in ks:
            entrain = profiles[0, k].astype(F32)
            start = aligned(k * rows, rows)
            for t in range(tracers):
                at = aligned((t * levels + k) * rows, rows)
                mixed[pl.ds(at, rows), :] = adj[pl.ds(at, rows), :] + entrain * mix[
                    pl.ds(start, rows), t * LANES : (t + 1) * LANES
                ]

    over_levels(levels, body)


def send_edges(dims, mixed, up, down, west, east):
    tracers, levels, rows = dims
    count = tracers * levels
    lat = lax.axis_index("lat")
    last = lax.axis_size("lat") - 1
    first_row = mixed[pl.ds(0, count, stride=rows), :]
    last_row = mixed[pl.ds(rows - 1, count, stride=rows), :]
    up[...] = jnp.where(lat < last, last_row, 0.0).astype(BF16)
    down[...] = jnp.where(lat > 0, first_row, 0.0).astype(BF16)
    lane = iota((rows, LANES), 1)
    sub = iota((rows, LANES), 0)
    pick = ((sub == 0) & (lane == 0)) | ((sub == 1) & (lane == LANES - 1))
    sides = dot_nt(pick.astype(BF16), mixed[...].astype(BF16))
    west[...] = sides[0:1]
    east[...] = sides[1:2]


def store_low(low, k2, rows, t, parts):
    low[pl.ds(aligned(k2 * 2 * rows, 2 * rows), 2 * rows), t * LANES : (t + 1) * LANES] = jnp.concatenate(
        parts, axis=0
    ).astype(BF16)


def over_levels(levels, body):
    for k2 in range(levels // 2):
        body(k2, (2 * k2, 2 * k2 + 1))
    if levels % 2:
        body(levels // 2, (levels - 1,))


def first_body(dims, kernel, profiles, adjoint, mixed, kron, up, down, west, east, low, mix):
    tracers, levels, rows = dims
    kron[...] = expand_kernel(kernel[...], levels, low.shape[0] // rows, rows)

    def body(k2, ks):
        detrains = [profiles[1, k].astype(F32) for k in ks]
        for t in range(tracers):
            parts = [
                d * adjoint[pl.ds(aligned((t * levels + k) * rows, rows), rows), :] for d, k in zip(detrains, ks)
            ]
            store_low(low, k2, rows, t, parts if len(parts) == 2 else parts + [jnp.zeros_like(parts[0])])

    over_levels(levels, body)
    convect(dims, adjoint, low, mix, kron, profiles, mixed)
    send_edges(dims, mixed, up, down, west, east)


def unpack_halo(dims, north, south, east, west, north_scr, south_scr, sides):
    tracers, levels, rows = dims
    count = tracers * levels
    north_scr[0:count, :] = north[...].astype(F32)
    south_scr[0:count, :] = south[...].astype(F32)
    sub = iota((rows, count * rows), 0)
    got = jnp.where(sub == 0, east[...], jnp.where(sub == 1, west[...], 0.0)).astype(BF16)
    lane = iota((rows, LANES), 1)
    sub = iota((rows, LANES), 0)
    place = (((sub == 0) & (lane == LANES - 1)) | ((sub == 1) & (lane == 0))).astype(BF16)
    sides[...] = dot_tn(got, place)


def transport(dims, k, fraction, mixed, north_scr, south_scr, sides):
    tracers, levels, rows = dims
    f = [fraction[0, d, k].astype(F32) for d in range(4)]
    remain = 1.0 - f[0] - f[1] - f[2] - f[3]
    lane = iota((rows, LANES), 1)
    sub = iota((rows, LANES), 0)
    out = []
    for t in range(tracers):
        index = t * levels + k
        at = pl.ds(aligned(index * rows, rows), rows)
        m = mixed[at, :]
        side = sides[at, :]
        east = jnp.where(lane == LANES - 1, side, pltpu.roll(m, LANES - 1, 1))
        west = jnp.where(lane == 0, side, pltpu.roll(m, 1, 1))
        north = jnp.where(
            sub == rows - 1,
            jnp.broadcast_to(north_scr[pl.ds(index, 1), :], (rows, LANES)),
            pltpu.roll(m, rows - 1, 0),
        )
        south = jnp.where(
            sub == 0, jnp.broadcast_to(south_scr[pl.ds(index, 1), :], (rows, LANES)), pltpu.roll(m, 1, 0)
        )
        out.append((at, remain * m + f[0] * east + f[1] * west + f[2] * north + f[3] * south))
    return out


def step_body(dims, mixed, north, south, east, west, fraction, profiles, kron, surface, *rest):
    new_mixed, up, down, to_west, to_east, new_surface, north_scr, south_scr, sides, adj, low, mix = rest
    tracers, levels, rows = dims
    unpack_halo(dims, north, south, east, west, north_scr, south_scr, sides)

    def body(k2, ks):
        parts = [[] for _ in range(tracers)]
        for k in ks:
            detrain = profiles[1, k].astype(F32)
            for t, (at, value) in enumerate(transport(dims, k, fraction, mixed, north_scr, south_scr, sides)):
                adj[at, :] = value
                parts[t].append(detrain * value)
        for t in range(tracers):
            two = parts[t] if len(ks) == 2 else parts[t] + [jnp.zeros_like(parts[t][0])]
            store_low(low, k2, rows, t, two)

    over_levels(levels, body)
    convect(dims, adj, low, mix, kron, profiles, new_mixed)
    send_edges(dims, new_mixed, up, down, to_west, to_east)
    for t in range(tracers):
        at = t * levels * rows
        new_surface[t * rows : (t + 1) * rows, :] = surface[t * rows : (t + 1) * rows, :] + adj[at : at + rows, :]


def last_body(dims, mixed, north, south, east, west, fraction, forcing, surface, *rest):
    adjoint, surface_low, north_scr, south_scr, sides = rest
    tracers, levels, rows = dims
    unpack_halo(dims, north, south, east, west, north_scr, south_scr, sides)

    def body(k2, ks):
        for k in ks:
            start = aligned(k * rows, rows)
            for t, (at, value) in enumerate(transport(dims, k, fraction, mixed, north_scr, south_scr, sides)):
                adjoint[at, :] = value + forcing[pl.ds(start, rows), t * LANES : (t + 1) * LANES]

    over_levels(levels, body)
    for t in range(tracers):
        at = t * levels * rows
        total = surface[t * rows : (t + 1) * rows, :] + adjoint[at : at + rows, :]
        surface_low[t * rows : (t + 1) * rows, :] = total.astype(BF16)


def pack_body(sizes, owner, count, cols, weights, resid, out):
    devices, blocks, slots, levels, tracers, chunk = sizes
    own = owner[...].astype(F32)
    wide = jnp.broadcast_to(own, (blocks, blocks))
    below = iota((blocks, blocks), 0)
    along = iota((blocks, blocks), 1)
    own_col = jnp.sum(jnp.where(below == along, wide, 0.0), axis=1, keepdims=True)
    earlier = jnp.where((own_col == wide) & (below < along), 1.0, 0.0)
    rank = jnp.sum(earlier, axis=0, keepdims=True)
    table = jnp.concatenate(
        [own, rank, count[...].astype(F32), jnp.zeros((5, blocks), F32)], axis=0
    ).astype(BF16)
    total = blocks * slots
    spread = (iota((blocks, total), 1) // slots == iota((blocks, total), 0)).astype(BF16)
    each = jnp.dot(table, spread, preferred_element_type=F32)
    slot = iota((1, total), 1) % slots
    target = (each[0:1].astype(jnp.int32) * CAPACITY + each[1:2].astype(jnp.int32)) * slots + slot
    valid = slot < each[2:3].astype(jnp.int32)
    held = jnp.where(valid, resid[...].astype(F32), 0.0)
    place = cols[...]
    high = (place // LANES).astype(F32)
    lower = (place % LANES).astype(F32)
    fill = LANES - levels - tracers - 2
    data = jnp.concatenate(
        [weights[...].astype(F32), held, high, lower, jnp.zeros((fill, total), F32)], axis=0
    ).astype(BF16)

    def body(c, carry):
        at = aligned(c * chunk, chunk)
        pick = jnp.where(iota((chunk, total), 0) + at == target, 1.0, 0.0).astype(BF16)
        out[pl.ds(at, chunk), :] = dot_nt(pick, data).astype(BF16)
        return carry

    lax.fori_loop(0, out.shape[0] // chunk, body, 0)


def forcing_body(dims, chunk, got, forcing, left, right):
    tracers, levels, rows = dims
    padded = left.shape[0] // rows

    def body(c, carry):
        at = aligned(c * chunk, chunk)
        part = got[pl.ds(at, chunk), :].astype(F32)
        lane = iota((chunk, LANES), 1).astype(F32)
        hit = part[:, levels + tracers + 1 : levels + tracers + 2] == lane
        for t in range(tracers):
            right[:, t * LANES : (t + 1) * LANES] = jnp.where(
                hit, part[:, levels + t : levels + t + 1], 0.0
            ).astype(BF16)
        turned = part.T
        high = turned[levels + tracers : levels + tracers + 1, :]
        sub = iota((rows, chunk), 0).astype(F32)
        mine = sub == high
        for k2 in range(padded // 2):
            two = []
            for k in (2 * k2, 2 * k2 + 1):
                two.append(jnp.where(mine, turned[k : k + 1, :], 0.0) if k < levels else jnp.zeros((rows, chunk), F32))
            left[2 * k2 * rows : (2 * k2 + 2) * rows, :] = jnp.concatenate(two, axis=0).astype(BF16)
        value = jnp.dot(left[...], right[...], preferred_element_type=F32)

        @pl.when(c == 0)
        def _():
            forcing[...] = value

        @pl.when(c > 0)
        def _():
            forcing[...] += value

        return carry

    lax.fori_loop(0, got.shape[0] // chunk, body, 0)


def lon_body(got, matrix, out):
    count = got.shape[0]
    total = jnp.zeros(out.shape, F32)
    for z in range(count):
        total = total + dot_nt(got[z], matrix[:, z * LANES : (z + 1) * LANES])
    out[...] = total.astype(BF16)


def lat_body(tracers, rows, got, matrix, out):
    bands = got.shape[0]
    size = tracers * rows
    lat = lax.axis_index("lat")
    own = matrix[pl.ds(aligned(lat * rows, rows), rows), :]
    own = jnp.concatenate([own] * tracers, axis=0)
    total = jnp.zeros(out.shape, F32)
    for b in range(bands):
        block = own[:, b * rows : (b + 1) * rows]
        block = jnp.concatenate([block] * tracers, axis=1)
        same = iota((size, size), 0) // rows == iota((size, size), 1) // rows
        total = total + jnp.dot(
            jnp.where(same, block, 0.0).astype(BF16), got[b], preferred_element_type=F32
        )
    out[...] = total


def ring(axis, step):
    count = lax.axis_size(axis)
    return [(i, (i + step) % count) for i in range(count)]


def exchange(up, down, to_west, to_east):
    south = lax.ppermute(up, "lat", ring("lat", 1))
    north = lax.ppermute(down, "lat", ring("lat", -1))
    east = lax.ppermute(to_west, "lon", ring("lon", -1))
    west = lax.ppermute(to_east, "lon", ring("lon", 1))
    return north, south, east, west


def shards(
    adjoint_in,
    fractions,
    profiles,
    kernel,
    obs_weights,
    obs_resid,
    obs_cols,
    obs_owner,
    obs_count,
    lat_matrix,
    lon_matrix,
):
    dims = tracers, levels, rows = adjoint_in.shape[:3]
    assert adjoint_in.shape[3] == LANES
    padded = (levels + 1) // 2 * 2
    count = tracers * levels
    cells = count * rows
    wide = tracers * LANES
    devices = lax.axis_size(BOTH)
    state = jax.ShapeDtypeStruct((cells, LANES), F32)
    row_edge = jax.ShapeDtypeStruct((count, LANES), BF16)
    side_edge = jax.ShapeDtypeStruct((1, cells), F32)
    edges = [row_edge, row_edge, side_edge, side_edge]
    kron_type = jax.ShapeDtypeStruct((padded * rows, padded * rows), BF16)
    surface_type = jax.ShapeDtypeStruct((tracers * rows, LANES), F32)
    low_scr = pltpu.VMEM((padded * rows, wide), BF16)
    mix_scr = pltpu.VMEM((padded * rows, wide), F32)
    halo_scr = [
        pltpu.VMEM(((count + 7) // 8 * 8, LANES), F32),
        pltpu.VMEM(((count + 7) // 8 * 8, LANES), F32),
        pltpu.VMEM((cells, LANES), F32),
    ]

    def spec(leaf):
        return full(leaf.shape)

    mixed, kron, *out = pl.pallas_call(
        functools.partial(first_body, dims),
        grid=(1,),
        out_shape=[state, kron_type] + edges,
        in_specs=[full(kernel.shape), full(profiles.shape), spec(state)],
        out_specs=[spec(s) for s in [state, kron_type] + edges],
        scratch_shapes=[low_scr, mix_scr],
        compiler_params=params(),
        name="first",
    )(kernel, profiles, adjoint_in.reshape(cells, LANES))
    halo = exchange(*out)

    blocks = obs_count.shape[0]
    slots = obs_cols.shape[0] // blocks
    rows_out = devices * CAPACITY * slots
    packed = pl.pallas_call(
        functools.partial(pack_body, (devices, blocks, slots, levels, tracers, 8 * CAPACITY * slots)),
        out_shape=jax.ShapeDtypeStruct((rows_out, LANES), BF16),
        compiler_params=params(),
        name="pack",
    )(
        obs_owner.reshape(1, blocks),
        obs_count.reshape(1, blocks),
        obs_cols.reshape(1, blocks * slots),
        obs_weights,
        obs_resid,
    )
    got = lax.all_to_all(
        packed.reshape(devices, CAPACITY * slots, LANES), BOTH, split_axis=0, concat_axis=0, tiled=True
    )
    chunk = min(rows_out, 1536)
    forcing = pl.pallas_call(
        functools.partial(forcing_body, dims, chunk),
        out_shape=jax.ShapeDtypeStruct((padded * rows, wide), F32),
        scratch_shapes=[pltpu.VMEM((padded * rows, chunk), BF16), pltpu.VMEM((chunk, wide), BF16)],
        compiler_params=params(),
        name="forcing",
    )(got.reshape(rows_out, LANES))

    surface = jnp.zeros(surface_type.shape, F32)
    for step_index in range(STEPS - 1, 0, -1):
        frac_spec = pl.BlockSpec((1,) + fractions.shape[1:], lambda i, n=step_index: (n, 0, 0, 0, 0))
        mixed, *out, surface = pl.pallas_call(
            functools.partial(step_body, dims),
            grid=(1,),
            out_shape=[state] + edges + [surface_type],
            in_specs=[spec(state), spec(row_edge), spec(row_edge), spec(side_edge), spec(side_edge)]
            + [frac_spec, full(profiles.shape), spec(kron_type), spec(surface_type)],
            out_specs=[spec(s) for s in [state] + edges + [surface_type]],
            scratch_shapes=halo_scr + [pltpu.VMEM((cells, LANES), F32), low_scr, mix_scr],
            compiler_params=params(),
            name="step",
        )(mixed, *halo, fractions, profiles, kron, surface)
        halo = exchange(*out)

    frac_spec = pl.BlockSpec((1,) + fractions.shape[1:], lambda i: (0, 0, 0, 0, 0))
    low_type = jax.ShapeDtypeStruct(surface_type.shape, BF16)
    adjoint, surface_low = pl.pallas_call(
        functools.partial(last_body, dims),
        grid=(1,),
        out_shape=[state, low_type],
        in_specs=[spec(state), spec(row_edge), spec(row_edge), spec(side_edge), spec(side_edge)]
        + [frac_spec, full(forcing.shape), spec(surface_type)],
        out_specs=[spec(state), spec(low_type)],
        scratch_shapes=halo_scr,
        compiler_params=params(),
        name="last",
    )(mixed, *halo, fractions, forcing, surface)

    lon_count = lax.axis_size("lon")
    spread = jnp.broadcast_to(surface_low[None], (lon_count,) + surface_low.shape)
    band = lax.all_to_all(spread, "lon", split_axis=0, concat_axis=0, tiled=True)
    across = pl.pallas_call(
        lon_body,
        out_shape=low_type,
        compiler_params=params(),
        name="lon_smooth",
    )(band, lon_matrix)
    column = lax.all_gather(across, "lat", axis=0)
    smoothed = pl.pallas_call(
        functools.partial(lat_body, tracers, rows),
        out_shape=surface_type,
        compiler_params=params(),
        name="lat_smooth",
    )(column, lat_matrix)
    return adjoint.reshape(adjoint_in.shape), smoothed.reshape(tracers, rows, LANES)


def solution(mesh):
    placed = (
        P(None, None, "lat", "lon"),
        P(None, None, None, "lat", "lon"),
        P(None, None, "lat", "lon"),
        P(),
        P(None, BOTH),
        P(None, BOTH),
        P(BOTH),
        P(BOTH, None),
        P(BOTH),
        P(),
        P("lon", None),
    )
    return jax.shard_map(
        shards,
        mesh=mesh,
        in_specs=placed,
        out_specs=(P(None, None, "lat", "lon"), P(None, "lat", "lon")),
        check_vma=False,
    )
```

```python
import functools

import jax
import jax.numpy as jnp
from jax import lax
from jax.experimental import pallas as pl
from jax.experimental.pallas import tpu as pltpu
from jax.sharding import PartitionSpec as P

STEPS = 4
CAPACITY = 6
F32 = jnp.float32
BF16 = jnp.bfloat16
BOTH = ("lat", "lon")
LANES = 128


def aligned(value, by):
    return value if isinstance(value, int) else pl.multiple_of(value, by)


def iota(shape, dim):
    return lax.broadcasted_iota(jnp.int32, shape, dim)


def dot_nt(a, b):
    return lax.dot_general(a, b, (((1,), (1,)), ((), ())), preferred_element_type=F32)


def dot_tn(a, b):
    return lax.dot_general(a, b, (((0,), (0,)), ((), ())), preferred_element_type=F32)


def full(shape):
    return pl.BlockSpec(shape, lambda i: (0,) * len(shape))


def params(limit=48 << 20):
    return pltpu.CompilerParams(vmem_limit_bytes=limit)


def expand_kernel(kernel, levels, padded, rows):
    size = padded * rows
    spread = (iota((size, levels), 0) // rows == iota((size, levels), 1)).astype(BF16)
    half = dot_nt(spread, kernel).astype(BF16)
    whole = dot_nt(half, spread)
    same = iota((size, size), 0) % rows == iota((size, size), 1) % rows
    return jnp.where(same, whole, 0.0).astype(BF16)


def convect(dims, adj, low, mix, kron, profiles, mixed):
    tracers, levels, rows = dims
    mix[...] = jnp.dot(kron[...], low[...], preferred_element_type=F32)

    def body(k2, ks):
        for k in ks:
            entrain = profiles[0, k].astype(F32)
            start = aligned(k * rows, rows)
            for t in range(tracers):
                at = aligned((t * levels + k) * rows, rows)
                mixed[pl.ds(at, rows), :] = adj[pl.ds(at, rows), :] + entrain * mix[
                    pl.ds(start, rows), t * LANES : (t + 1) * LANES
                ]

    over_levels(levels, body)


def end_columns(rows_2d):
    lane = iota((8, LANES), 1)
    sub = iota((8, LANES), 0)
    pick = ((sub == 0) & (lane == 0)) | ((sub == 1) & (lane == LANES - 1))
    return dot_nt(pick.astype(BF16), rows_2d.astype(BF16))


def spread_columns(first, last):
    lane = iota((8, LANES), 1)
    sub = iota((8, first.shape[1]), 0)
    got = jnp.where(sub == 0, last, jnp.where(sub == 1, first, 0.0)).astype(BF16)
    sub = iota((8, LANES), 0)
    place = (((sub == 0) & (lane == LANES - 1)) | ((sub == 1) & (lane == 0))).astype(BF16)
    return dot_tn(got, place)


def send_edges(dims, mixed, up, down, west, east):
    tracers, levels, rows = dims
    count = tracers * levels
    lat = lax.axis_index("lat")
    last = lax.axis_size("lat") - 1
    first_row = mixed[pl.ds(0, count, stride=rows), :]
    last_row = mixed[pl.ds(rows - 1, count, stride=rows), :]
    up[0:count, :] = jnp.where(lat < last, last_row, 0.0).astype(BF16)
    down[0:count, :] = jnp.where(lat > 0, first_row, 0.0).astype(BF16)
    sides = end_columns(mixed[...])
    west[:, 0 : count * rows] = sides[0:1]
    east[:, 0 : count * rows] = sides[1:2]


def store_low(low, k2, rows, t, parts):
    low[pl.ds(aligned(k2 * 2 * rows, 2 * rows), 2 * rows), t * LANES : (t + 1) * LANES] = jnp.concatenate(
        parts, axis=0
    ).astype(BF16)


def over_levels(levels, body):
    for k2 in range(levels // 2):
        body(k2, (2 * k2, 2 * k2 + 1))
    if levels % 2:
        body(levels // 2, (levels - 1,))


def first_body(dims, kernel, profiles, adjoint, fraction, mixed, kron, up, down, west, east, low, mix):
    tracers, levels, rows = dims
    kron[...] = expand_kernel(kernel[...], levels, low.shape[0] // rows, rows)

    def body(k2, ks):
        detrains = [profiles[1, k].astype(F32) for k in ks]
        for t in range(tracers):
            parts = [
                d * adjoint[pl.ds(aligned((t * levels + k) * rows, rows), rows), :] for d, k in zip(detrains, ks)
            ]
            store_low(low, k2, rows, t, parts if len(parts) == 2 else parts + [jnp.zeros_like(parts[0])])

    over_levels(levels, body)
    convect(dims, adjoint, low, mix, kron, profiles, mixed)
    send_edges(dims, mixed, up, down, west, east)
    count = tracers * levels
    lat = lax.axis_index("lat")
    last = lax.axis_size("lat") - 1
    f = [fraction[0, d, 0].astype(F32) for d in range(4)]
    pad = jnp.zeros((up.shape[0] - count - 1, LANES), F32)
    up[count:, :] = jnp.concatenate([jnp.where(lat < last, f[2][rows - 1 :], 0.0), pad], axis=0).astype(BF16)
    down[count:, :] = jnp.concatenate([jnp.where(lat > 0, f[3][:1], 0.0), pad], axis=0).astype(BF16)
    at = (count * rows + LANES - 1) // LANES * LANES
    west[:, at : at + tracers * rows] = end_columns(jnp.concatenate([f[1]] * tracers, axis=0))[0:1]
    east[:, at : at + tracers * rows] = end_columns(jnp.concatenate([f[0]] * tracers, axis=0))[1:2]


def unpack_halo(dims, north, south, east, west, north_scr, south_scr, sides):
    tracers, levels, rows = dims
    count = tracers * levels
    north_scr[0:count, :] = north[0:count, :].astype(F32)
    south_scr[0:count, :] = south[0:count, :].astype(F32)
    sides[...] = spread_columns(west[:, 0 : count * rows], east[:, 0 : count * rows])


def transport(dims, k, fraction, mixed, north_scr, south_scr, sides):
    tracers, levels, rows = dims
    f = [fraction[0, d, k].astype(F32) for d in range(4)]
    remain = 1.0 - f[0] - f[1] - f[2] - f[3]
    lane = iota((rows, LANES), 1)
    sub = iota((rows, LANES), 0)
    out = []
    for t in range(tracers):
        index = t * levels + k
        at = pl.ds(aligned(index * rows, rows), rows)
        m = mixed[at, :]
        side = sides[at, :]
        east = jnp.where(lane == LANES - 1, side, pltpu.roll(m, LANES - 1, 1))
        west = jnp.where(lane == 0, side, pltpu.roll(m, 1, 1))
        north = jnp.where(
            sub == rows - 1,
            jnp.broadcast_to(north_scr[pl.ds(index, 1), :], (rows, LANES)),
            pltpu.roll(m, rows - 1, 0),
        )
        south = jnp.where(
            sub == 0, jnp.broadcast_to(south_scr[pl.ds(index, 1), :], (rows, LANES)), pltpu.roll(m, 1, 0)
        )
        out.append((at, remain * m + f[0] * east + f[1] * west + f[2] * north + f[3] * south))
    return out


def step_body(dims, last, mixed, north, south, east, west, fraction, profiles, kron, surface, *rest):
    if last:
        extra, rest = rest[:6], rest[6:]
    new_mixed, up, down, to_west, to_east, new_surface, north_scr, south_scr, sides, adj, low, mix = rest
    tracers, levels, rows = dims
    unpack_halo(dims, north, south, east, west, north_scr, south_scr, sides)

    def body(k2, ks):
        parts = [[] for _ in range(tracers)]
        for k in ks:
            detrain = profiles[1, k].astype(F32)
            for t, (at, value) in enumerate(transport(dims, k, fraction, mixed, north_scr, south_scr, sides)):
                adj[at, :] = value
                parts[t].append(detrain * value)
        for t in range(tracers):
            two = parts[t] if len(ks) == 2 else parts[t] + [jnp.zeros_like(parts[t][0])]
            store_low(low, k2, rows, t, two)

    over_levels(levels, body)
    convect(dims, adj, low, mix, kron, profiles, new_mixed)
    send_edges(dims, new_mixed, up, down, to_west, to_east)
    total = [
        surface[t * rows : (t + 1) * rows, :] + adj[t * levels * rows : t * levels * rows + rows, :]
        for t in range(tracers)
    ]
    if last:
        patch(dims, new_mixed, total, *extra, new_surface)
    else:
        new_surface[...] = jnp.concatenate(total, axis=0)


def patch(dims, mixed, total, fraction, forcing, north, south, east, west, out):
    tracers, levels, rows = dims
    count = tracers * levels
    f = [fraction[0, d, 0].astype(F32) for d in range(4)]
    remain = 1.0 - f[0] - f[1] - f[2] - f[3]
    lane = iota((rows, LANES), 1)
    sub = iota((rows, LANES), 0)
    below = south[count : count + 8, :].astype(F32)[0:1]
    above = north[count : count + 8, :].astype(F32)[0:1]
    tile, under, over = [], [], []
    for t in range(tracers):
        m = mixed[t * levels * rows : t * levels * rows + rows, :]
        value = remain * m
        value = value + f[0] * jnp.where(lane == LANES - 1, 0.0, pltpu.roll(m, LANES - 1, 1))
        value = value + f[1] * jnp.where(lane == 0, 0.0, pltpu.roll(m, 1, 1))
        value = value + f[2] * jnp.where(sub == rows - 1, 0.0, pltpu.roll(m, rows - 1, 0))
        value = value + f[3] * jnp.where(sub == 0, 0.0, pltpu.roll(m, 1, 0))
        tile.append(total[t] + value + forcing[0:rows, t * LANES : (t + 1) * LANES])
        under.append(below * m[0:1])
        over.append(above * m[rows - 1 : rows])
    tops = jnp.concatenate([mixed[t * levels * rows : t * levels * rows + rows, :] for t in range(tracers)], axis=0)
    columns = end_columns(tops)
    at = (count * rows + LANES - 1) // LANES * LANES
    size = tracers * rows
    to_west = columns[0:1] * west[:, at : at + size]
    to_east = columns[1:2] * east[:, at : at + size]
    ends = jnp.concatenate([to_west, to_east, jnp.zeros((6, size), F32)], axis=0)
    ends = jnp.concatenate([ends, jnp.zeros((8, LANES - size), F32)], axis=1)
    short = (-2 * tracers) % 8
    filler = [jnp.zeros((short, LANES), F32)] if short else []
    whole = jnp.concatenate(tile + under + over + filler + [ends], axis=0)
    for z in range(out.shape[0]):
        out[z] = whole.astype(BF16)


def last_body(dims, mixed, north, south, east, west, fraction, forcing, *rest):
    adjoint, north_scr, south_scr, sides = rest
    tracers, levels, rows = dims
    unpack_halo(dims, north, south, east, west, north_scr, south_scr, sides)

    def body(k2, ks):
        for k in ks:
            start = aligned(k * rows, rows)
            for t, (at, value) in enumerate(transport(dims, k, fraction, mixed, north_scr, south_scr, sides)):
                adjoint[at, :] = value + forcing[pl.ds(start, rows), t * LANES : (t + 1) * LANES]

    over_levels(levels, body)


def pack_body(sizes, owner, count, cols, weights, resid, out):
    devices, blocks, slots, levels, tracers, chunk = sizes
    own = owner[...].astype(F32)
    wide = jnp.broadcast_to(own, (blocks, blocks))
    below = iota((blocks, blocks), 0)
    along = iota((blocks, blocks), 1)
    own_col = jnp.sum(jnp.where(below == along, wide, 0.0), axis=1, keepdims=True)
    earlier = jnp.where((own_col == wide) & (below < along), 1.0, 0.0)
    rank = jnp.sum(earlier, axis=0, keepdims=True)
    table = jnp.concatenate(
        [own, rank, count[...].astype(F32), jnp.zeros((5, blocks), F32)], axis=0
    ).astype(BF16)
    total = blocks * slots
    spread = (iota((blocks, total), 1) // slots == iota((blocks, total), 0)).astype(BF16)
    each = jnp.dot(table, spread, preferred_element_type=F32)
    slot = iota((1, total), 1) % slots
    target = (each[0:1].astype(jnp.int32) * CAPACITY + each[1:2].astype(jnp.int32)) * slots + slot
    valid = slot < each[2:3].astype(jnp.int32)
    held = jnp.where(valid, resid[...].astype(F32), 0.0)
    place = cols[...]
    high = (place // LANES).astype(F32)
    lower = (place % LANES).astype(F32)
    fill = LANES - levels - tracers - 2
    data = jnp.concatenate(
        [weights[...].astype(F32), held, high, lower, jnp.zeros((fill, total), F32)], axis=0
    ).astype(BF16)

    def body(c, carry):
        at = aligned(c * chunk, chunk)
        pick = jnp.where(iota((chunk, total), 0) + at == target, 1.0, 0.0).astype(BF16)
        out[pl.ds(at, chunk), :] = dot_nt(pick, data).astype(BF16)
        return carry

    lax.fori_loop(0, out.shape[0] // chunk, body, 0)


def forcing_body(dims, chunk, got, forcing, left, right):
    tracers, levels, rows = dims
    padded = left.shape[0] // rows

    def body(c, carry):
        at = aligned(c * chunk, chunk)
        part = got[pl.ds(at, chunk), :].astype(F32)
        lane = iota((chunk, LANES), 1).astype(F32)
        hit = part[:, levels + tracers + 1 : levels + tracers + 2] == lane
        for t in range(tracers):
            right[:, t * LANES : (t + 1) * LANES] = jnp.where(
                hit, part[:, levels + t : levels + t + 1], 0.0
            ).astype(BF16)
        turned = part.T
        high = turned[levels + tracers : levels + tracers + 1, :]
        sub = iota((rows, chunk), 0).astype(F32)
        mine = sub == high
        for k2 in range(padded // 2):
            two = []
            for k in (2 * k2, 2 * k2 + 1):
                two.append(jnp.where(mine, turned[k : k + 1, :], 0.0) if k < levels else jnp.zeros((rows, chunk), F32))
            left[2 * k2 * rows : (2 * k2 + 2) * rows, :] = jnp.concatenate(two, axis=0).astype(BF16)
        value = jnp.dot(left[...], right[...], preferred_element_type=F32)

        @pl.when(c == 0)
        def _():
            forcing[...] = value

        @pl.when(c > 0)
        def _():
            forcing[...] += value

        return carry

    lax.fori_loop(0, got.shape[0] // chunk, body, 0)


def lon_body(size, got, matrix, out):
    count = got.shape[0]
    body = out.shape[0]
    total = jnp.zeros(out.shape, F32)
    ends = [got[z, body : body + 8, :].astype(F32)[:, 0:size] for z in range(count)]
    for z in range(count):
        side = spread_columns(ends[(z - 1) % count][1:2], ends[(z + 1) % count][0:1])
        block = got[z, 0:body, :].astype(F32)
        block = jnp.concatenate([block[0:size] + side, block[size:]], axis=0)
        total = total + dot_nt(block.astype(BF16), matrix[:, z * LANES : (z + 1) * LANES])
    out[...] = total.astype(BF16)


def lat_body(tracers, rows, got, matrix, out):
    bands = got.shape[0]
    size = tracers * rows
    extra = got.shape[1] - size
    lat = lax.axis_index("lat")
    own = matrix[pl.ds(pl.multiple_of(lat * rows, rows), rows), :].astype(F32)
    own = jnp.concatenate([own] * tracers, axis=0)
    tracer = iota((size, extra), 0) // rows
    column = iota((size, extra), 1)
    same = iota((size, size), 0) // rows == iota((size, size), 1) // rows
    total = jnp.zeros(out.shape, F32)
    for b in range(bands):
        block = jnp.concatenate([own[:, b * rows : (b + 1) * rows]] * tracers, axis=1)
        block = jnp.where(same, block, 0.0)
        under = max(b * rows - 1, 0)
        over = min((b + 1) * rows, bands * rows - 1)
        ring_part = jnp.where(column == tracer, own[:, under : under + 1], 0.0)
        ring_part = ring_part + jnp.where(column == tracer + tracers, own[:, over : over + 1], 0.0)
        weights = jnp.concatenate([block, ring_part], axis=1).astype(BF16)
        total = total + jnp.dot(weights, got[b], preferred_element_type=F32)
    out[...] = total


def ring(axis, step):
    count = lax.axis_size(axis)
    return [(i, (i + step) % count) for i in range(count)]


def exchange(up, down, to_west, to_east):
    south = lax.ppermute(up, "lat", ring("lat", 1))
    north = lax.ppermute(down, "lat", ring("lat", -1))
    east = lax.ppermute(to_west, "lon", ring("lon", -1))
    west = lax.ppermute(to_east, "lon", ring("lon", 1))
    return north, south, east, west


def shards(
    adjoint_in,
    fractions,
    profiles,
    kernel,
    obs_weights,
    obs_resid,
    obs_cols,
    obs_owner,
    obs_count,
    lat_matrix,
    lon_matrix,
):
    dims = tracers, levels, rows = adjoint_in.shape[:3]
    assert adjoint_in.shape[3] == LANES
    padded = (levels + 1) // 2 * 2
    count = tracers * levels
    cells = count * rows
    wide = tracers * LANES
    devices = lax.axis_size(BOTH)
    state = jax.ShapeDtypeStruct((cells, LANES), F32)
    row_edge = jax.ShapeDtypeStruct((count, LANES), BF16)
    side_edge = jax.ShapeDtypeStruct((1, cells), F32)
    edges = [row_edge, row_edge, side_edge, side_edge]
    long_row = jax.ShapeDtypeStruct((count + 16, LANES), BF16)
    long_side = jax.ShapeDtypeStruct((1, (cells + LANES - 1) // LANES * LANES + LANES), F32)
    long_edges = [long_row, long_row, long_side, long_side]
    level_zero = pl.BlockSpec((1, 4, 1, rows, LANES), lambda i: (0, 0, 0, 0, 0))
    kron_type = jax.ShapeDtypeStruct((padded * rows, padded * rows), BF16)
    surface_type = jax.ShapeDtypeStruct((tracers * rows, LANES), F32)
    low_scr = pltpu.VMEM((padded * rows, wide), BF16)
    mix_scr = pltpu.VMEM((padded * rows, wide), F32)
    halo_scr = [
        pltpu.VMEM(((count + 7) // 8 * 8, LANES), F32),
        pltpu.VMEM(((count + 7) // 8 * 8, LANES), F32),
        pltpu.VMEM((cells, LANES), F32),
    ]

    def spec(leaf):
        return full(leaf.shape)

    mixed, kron, *out = pl.pallas_call(
        functools.partial(first_body, dims),
        grid=(1,),
        out_shape=[state, kron_type] + long_edges,
        in_specs=[full(kernel.shape), full(profiles.shape), spec(state), level_zero],
        out_specs=[spec(s) for s in [state, kron_type] + long_edges],
        scratch_shapes=[low_scr, mix_scr],
        compiler_params=params(),
        name="first",
    )(kernel, profiles, adjoint_in.reshape(cells, LANES), fractions)
    halo = first_halo = exchange(*out)
    obs_count, _ = lax.optimization_barrier((obs_count, out[2]))

    blocks = obs_count.shape[0]
    slots = obs_cols.shape[0] // blocks
    rows_out = devices * CAPACITY * slots
    packed = pl.pallas_call(
        functools.partial(pack_body, (devices, blocks, slots, levels, tracers, 8 * CAPACITY * slots)),
        grid=(1,),
        out_shape=jax.ShapeDtypeStruct((rows_out, LANES), BF16),
        in_specs=[
            full((1, blocks)),
            full((1, blocks)),
            full((1, blocks * slots)),
            full(obs_weights.shape),
            full(obs_resid.shape),
        ],
        out_specs=full((rows_out, LANES)),
        compiler_params=params(60 << 20),
        name="pack",
    )(
        obs_owner.reshape(1, blocks),
        obs_count.reshape(1, blocks),
        obs_cols.reshape(1, blocks * slots),
        obs_weights,
        obs_resid,
    )
    got = lax.all_to_all(
        packed.reshape(devices, CAPACITY * slots, LANES), BOTH, split_axis=0, concat_axis=0, tiled=True
    )
    chunk = min(rows_out, 1536)
    forcing = pl.pallas_call(
        functools.partial(forcing_body, dims, chunk),
        out_shape=jax.ShapeDtypeStruct((padded * rows, wide), F32),
        scratch_shapes=[pltpu.VMEM((padded * rows, chunk), BF16), pltpu.VMEM((chunk, wide), BF16)],
        compiler_params=params(),
        name="forcing",
    )(got.reshape(rows_out, LANES))

    surface = jnp.zeros(surface_type.shape, F32)
    lon_count = lax.axis_size("lon")
    patch_rows = (tracers * (rows + 2) + 7) // 8 * 8
    patch_type = jax.ShapeDtypeStruct((lon_count, patch_rows + 8, LANES), BF16)
    for step_index in range(STEPS - 1, 0, -1):
        last = step_index == 1
        frac_spec = pl.BlockSpec((1,) + fractions.shape[1:], lambda i, n=step_index: (n, 0, 0, 0, 0))
        halo_types = long_edges if step_index == STEPS - 1 else edges
        ins = [mixed, *halo, fractions, profiles, kron, surface]
        in_specs = [spec(state)] + [spec(h) for h in halo_types]
        in_specs += [frac_spec, full(profiles.shape), spec(kron_type), spec(surface_type)]
        result = surface_type
        if last:
            ins += [fractions, forcing, *first_halo]
            in_specs += [level_zero, pl.BlockSpec((rows, wide), lambda i: (0, 0))] + [spec(h) for h in long_edges]
            result = patch_type
        mixed, *out, surface = pl.pallas_call(
            functools.partial(step_body, dims, last),
            grid=(1,),
            out_shape=[state] + edges + [result],
            in_specs=in_specs,
            out_specs=[spec(s) for s in [state] + edges + [result]],
            scratch_shapes=halo_scr + [pltpu.VMEM((cells, LANES), F32), low_scr, mix_scr],
            compiler_params=params(),
            name="step",
        )(*ins)
        halo = exchange(*out)

    band = lax.all_to_all(surface, "lon", split_axis=0, concat_axis=0, tiled=True)
    frac_spec = pl.BlockSpec((1,) + fractions.shape[1:], lambda i: (0, 0, 0, 0, 0))
    adjoint = pl.pallas_call(
        functools.partial(last_body, dims),
        grid=(1,),
        out_shape=state,
        in_specs=[spec(state)] + [spec(h) for h in edges] + [frac_spec, full(forcing.shape)],
        out_specs=spec(state),
        scratch_shapes=halo_scr,
        compiler_params=params(),
        name="last",
    )(mixed, *halo, fractions, forcing)

    across = pl.pallas_call(
        functools.partial(lon_body, tracers * rows),
        out_shape=jax.ShapeDtypeStruct((patch_rows, LANES), BF16),
        compiler_params=params(),
        name="lon_smooth",
    )(band, lon_matrix)
    column = lax.all_gather(across, "lat", axis=0)
    smoothed = pl.pallas_call(
        functools.partial(lat_body, tracers, rows),
        out_shape=surface_type,
        compiler_params=params(),
        name="lat_smooth",
    )(column, lat_matrix)
    return adjoint.reshape(adjoint_in.shape), smoothed.reshape(tracers, rows, LANES)


def solution(mesh):
    placed = (
        P(None, None, "lat", "lon"),
        P(None, None, None, "lat", "lon"),
        P(None, None, "lat", "lon"),
        P(),
        P(None, BOTH),
        P(None, BOTH),
        P(BOTH),
        P(BOTH, None),
        P(BOTH),
        P(),
        P("lon", None),
    )
    return jax.shard_map(
        shards,
        mesh=mesh,
        in_specs=placed,
        out_specs=(P(None, None, "lat", "lon"), P(None, "lat", "lon")),
        check_vma=False,
    )
```

```python
import functools

import jax
import jax.numpy as jnp
from jax import lax
from jax.experimental import pallas as pl
from jax.experimental.pallas import tpu as pltpu
from jax.sharding import PartitionSpec as P

STEPS = 4
CAPACITY = 6
F32 = jnp.float32
BF16 = jnp.bfloat16
BOTH = ("lat", "lon")
LANES = 128


def aligned(value, by):
    return value if isinstance(value, int) else pl.multiple_of(value, by)


def iota(shape, dim):
    return lax.broadcasted_iota(jnp.int32, shape, dim)


def dot_nt(a, b):
    return lax.dot_general(a, b, (((1,), (1,)), ((), ())), preferred_element_type=F32)


def dot_tn(a, b):
    return lax.dot_general(a, b, (((0,), (0,)), ((), ())), preferred_element_type=F32)


def full(shape):
    return pl.BlockSpec(shape, lambda i: (0,) * len(shape))


def params(limit=24 << 20):
    return pltpu.CompilerParams(vmem_limit_bytes=limit)


def expand_kernel(kernel, levels, padded, rows):
    size = padded * rows
    spread = (iota((size, levels), 0) // rows == iota((size, levels), 1)).astype(BF16)
    half = dot_nt(spread, kernel).astype(BF16)
    whole = dot_nt(half, spread)
    same = iota((size, size), 0) % rows == iota((size, size), 1) % rows
    return jnp.where(same, whole, 0.0).astype(BF16)


def convect(dims, adj, low, mix, kron, profiles, mixed):
    tracers, levels, rows = dims
    mix[...] = jnp.dot(kron[...], low[...], preferred_element_type=F32)

    def body(k2, ks):
        for k in ks:
            entrain = profiles[0, k].astype(F32)
            start = aligned(k * rows, rows)
            for t in range(tracers):
                at = aligned((t * levels + k) * rows, rows)
                mixed[pl.ds(at, rows), :] = adj[pl.ds(at, rows), :] + entrain * mix[
                    pl.ds(start, rows), t * LANES : (t + 1) * LANES
                ]

    over_levels(levels, body)


def end_columns(rows_2d):
    lane = iota((8, LANES), 1)
    sub = iota((8, LANES), 0)
    pick = ((sub == 0) & (lane == 0)) | ((sub == 1) & (lane == LANES - 1))
    return dot_nt(pick.astype(BF16), rows_2d.astype(BF16))


def spread_columns(first, last):
    lane = iota((8, LANES), 1)
    sub = iota((8, first.shape[1]), 0)
    got = jnp.where(sub == 0, last, jnp.where(sub == 1, first, 0.0)).astype(BF16)
    sub = iota((8, LANES), 0)
    place = (((sub == 0) & (lane == LANES - 1)) | ((sub == 1) & (lane == 0))).astype(BF16)
    return dot_tn(got, place)


def send_edges(dims, mixed, up, down, west, east):
    tracers, levels, rows = dims
    count = tracers * levels
    lat = lax.axis_index("lat")
    last = lax.axis_size("lat") - 1
    first_row = mixed[pl.ds(0, count, stride=rows), :]
    last_row = mixed[pl.ds(rows - 1, count, stride=rows), :]
    up[0:count, :] = jnp.where(lat < last, last_row, 0.0).astype(BF16)
    down[0:count, :] = jnp.where(lat > 0, first_row, 0.0).astype(BF16)
    sides = end_columns(mixed[...])
    west[:, 0 : count * rows] = sides[0:1]
    east[:, 0 : count * rows] = sides[1:2]


def store_low(low, k2, rows, t, parts):
    low[pl.ds(aligned(k2 * 2 * rows, 2 * rows), 2 * rows), t * LANES : (t + 1) * LANES] = jnp.concatenate(
        parts, axis=0
    ).astype(BF16)


def over_levels(levels, body):
    for k2 in range(levels // 2):
        body(k2, (2 * k2, 2 * k2 + 1))
    if levels % 2:
        body(levels // 2, (levels - 1,))


def first_body(dims, kernel, profiles, adjoint, fraction, mixed_out, kron_out, up, down, west, east, *rest):
    low, mix, mixed, kron, mixed_sem, kron_sem = rest
    tracers, levels, rows = dims
    kron[...] = expand_kernel(kernel[...], levels, low.shape[0] // rows, rows)
    kron_copy = pltpu.make_async_copy(kron, kron_out, kron_sem)
    kron_copy.start()

    def body(k2, ks):
        detrains = [profiles[1, k].astype(F32) for k in ks]
        for t in range(tracers):
            parts = [
                d * adjoint[pl.ds(aligned((t * levels + k) * rows, rows), rows), :] for d, k in zip(detrains, ks)
            ]
            store_low(low, k2, rows, t, parts if len(parts) == 2 else parts + [jnp.zeros_like(parts[0])])

    over_levels(levels, body)
    convect(dims, adjoint, low, mix, kron, profiles, mixed)
    mixed_copy = pltpu.make_async_copy(mixed, mixed_out, mixed_sem)
    mixed_copy.start()
    send_edges(dims, mixed, up, down, west, east)
    count = tracers * levels
    lat = lax.axis_index("lat")
    last = lax.axis_size("lat") - 1
    f = [fraction[0, d, 0].astype(F32) for d in range(4)]
    pad = jnp.zeros((up.shape[0] - count - 1, LANES), F32)
    up[count:, :] = jnp.concatenate([jnp.where(lat < last, f[2][rows - 1 :], 0.0), pad], axis=0).astype(BF16)
    down[count:, :] = jnp.concatenate([jnp.where(lat > 0, f[3][:1], 0.0), pad], axis=0).astype(BF16)
    at = (count * rows + LANES - 1) // LANES * LANES
    west[:, at : at + tracers * rows] = end_columns(jnp.concatenate([f[1]] * tracers, axis=0))[0:1]
    east[:, at : at + tracers * rows] = end_columns(jnp.concatenate([f[0]] * tracers, axis=0))[1:2]
    kron_copy.wait()
    mixed_copy.wait()


def unpack_halo(dims, north, south, east, west, north_scr, south_scr, sides):
    tracers, levels, rows = dims
    count = tracers * levels
    north_scr[0:count, :] = north[0:count, :].astype(F32)
    south_scr[0:count, :] = south[0:count, :].astype(F32)
    sides[...] = spread_columns(west[:, 0 : count * rows], east[:, 0 : count * rows])


def transport(dims, k, fraction, mixed, north_scr, south_scr, sides):
    tracers, levels, rows = dims
    f = [fraction[0, d, k].astype(F32) for d in range(4)]
    remain = 1.0 - f[0] - f[1] - f[2] - f[3]
    lane = iota((rows, LANES), 1)
    sub = iota((rows, LANES), 0)
    out = []
    for t in range(tracers):
        index = t * levels + k
        at = pl.ds(aligned(index * rows, rows), rows)
        m = mixed[at, :]
        side = sides[at, :]
        east = jnp.where(lane == LANES - 1, side, pltpu.roll(m, LANES - 1, 1))
        west = jnp.where(lane == 0, side, pltpu.roll(m, 1, 1))
        north = jnp.where(
            sub == rows - 1,
            jnp.broadcast_to(north_scr[pl.ds(index, 1), :], (rows, LANES)),
            pltpu.roll(m, rows - 1, 0),
        )
        south = jnp.where(
            sub == 0, jnp.broadcast_to(south_scr[pl.ds(index, 1), :], (rows, LANES)), pltpu.roll(m, 1, 0)
        )
        out.append((at, remain * m + f[0] * east + f[1] * west + f[2] * north + f[3] * south))
    return out


def step_body(dims, last, mixed, north, south, east, west, fraction, profiles, kron, surface, *rest):
    if last:
        extra, rest = rest[:6], rest[6:]
    new_mixed, up, down, to_west, to_east, new_surface, north_scr, south_scr, sides, adj, low, mix = rest
    tracers, levels, rows = dims
    unpack_halo(dims, north, south, east, west, north_scr, south_scr, sides)

    def body(k2, ks):
        parts = [[] for _ in range(tracers)]
        for k in ks:
            detrain = profiles[1, k].astype(F32)
            for t, (at, value) in enumerate(transport(dims, k, fraction, mixed, north_scr, south_scr, sides)):
                adj[at, :] = value
                parts[t].append(detrain * value)
        for t in range(tracers):
            two = parts[t] if len(ks) == 2 else parts[t] + [jnp.zeros_like(parts[t][0])]
            store_low(low, k2, rows, t, two)

    over_levels(levels, body)
    convect(dims, adj, low, mix, kron, profiles, new_mixed)
    send_edges(dims, new_mixed, up, down, to_west, to_east)
    total = [
        surface[t * rows : (t + 1) * rows, :] + adj[t * levels * rows : t * levels * rows + rows, :]
        for t in range(tracers)
    ]
    if last:
        patch(dims, new_mixed, total, *extra, new_surface)
        at = up.shape[0] - new_surface.shape[0]
        up[at:, :] = new_surface[...]
        down[at:, :] = new_surface[...]
    else:
        new_surface[...] = jnp.concatenate(total, axis=0)


def patch(dims, mixed, total, fraction, forcing, north, south, east, west, out):
    tracers, levels, rows = dims
    count = tracers * levels
    f = [fraction[0, d, 0].astype(F32) for d in range(4)]
    remain = 1.0 - f[0] - f[1] - f[2] - f[3]
    lane = iota((rows, LANES), 1)
    sub = iota((rows, LANES), 0)
    below = south[count : count + 8, :].astype(F32)[0:1]
    above = north[count : count + 8, :].astype(F32)[0:1]
    tile, under, over = [], [], []
    for t in range(tracers):
        m = mixed[t * levels * rows : t * levels * rows + rows, :]
        value = remain * m
        value = value + f[0] * jnp.where(lane == LANES - 1, 0.0, pltpu.roll(m, LANES - 1, 1))
        value = value + f[1] * jnp.where(lane == 0, 0.0, pltpu.roll(m, 1, 1))
        value = value + f[2] * jnp.where(sub == rows - 1, 0.0, pltpu.roll(m, rows - 1, 0))
        value = value + f[3] * jnp.where(sub == 0, 0.0, pltpu.roll(m, 1, 0))
        tile.append(total[t] + value + forcing[0:rows, t * LANES : (t + 1) * LANES])
        under.append(below * m[0:1])
        over.append(above * m[rows - 1 : rows])
    tops = jnp.concatenate([mixed[t * levels * rows : t * levels * rows + rows, :] for t in range(tracers)], axis=0)
    columns = end_columns(tops)
    at = (count * rows + LANES - 1) // LANES * LANES
    size = tracers * rows
    to_west = columns[0:1] * west[:, at : at + size]
    to_east = columns[1:2] * east[:, at : at + size]
    ends = jnp.concatenate([to_west, to_east, jnp.zeros((6, size), F32)], axis=0)
    ends = jnp.concatenate([ends, jnp.zeros((8, LANES - size), F32)], axis=1)
    short = (-2 * tracers) % 8
    filler = [jnp.zeros((short, LANES), F32)] if short else []
    whole = jnp.concatenate(tile + under + over + filler + [ends], axis=0)
    out[...] = whole.astype(BF16)


def last_body(dims, mixed, north, south, east, west, fraction, forcing, *rest):
    adjoint, north_scr, south_scr, sides = rest
    _, levels, rows = dims
    unpack_halo(dims, north, south, east, west, north_scr, south_scr, sides)

    def body(k2, ks):
        for k in ks:
            start = aligned(k * rows, rows)
            for t, (at, value) in enumerate(transport(dims, k, fraction, mixed, north_scr, south_scr, sides)):
                adjoint[at, :] = value + forcing[pl.ds(start, rows), t * LANES : (t + 1) * LANES]

    over_levels(levels, body)


def pack_body(sizes, owner, count, cols, weights, resid, out):
    _, blocks, slots, levels, tracers, chunk = sizes
    own = owner[...].astype(F32)
    wide = jnp.broadcast_to(own, (blocks, blocks))
    below = iota((blocks, blocks), 0)
    along = iota((blocks, blocks), 1)
    own_col = jnp.sum(jnp.where(below == along, wide, 0.0), axis=1, keepdims=True)
    earlier = jnp.where((own_col == wide) & (below < along), 1.0, 0.0)
    rank = jnp.sum(earlier, axis=0, keepdims=True)
    table = jnp.concatenate(
        [own, rank, count[...].astype(F32), jnp.zeros((5, blocks), F32)], axis=0
    ).astype(BF16)
    total = blocks * slots
    spread = (iota((blocks, total), 1) // slots == iota((blocks, total), 0)).astype(BF16)
    each = jnp.dot(table, spread, preferred_element_type=F32)
    slot = iota((1, total), 1) % slots
    target = (each[0:1].astype(jnp.int32) * CAPACITY + each[1:2].astype(jnp.int32)) * slots + slot
    valid = slot < each[2:3].astype(jnp.int32)
    held = jnp.where(valid, resid[...].astype(F32), 0.0)
    place = cols[...]
    high = (place // LANES).astype(F32)
    lower = (place % LANES).astype(F32)
    fill = LANES - levels - tracers - 2
    data = jnp.concatenate(
        [weights[...].astype(F32), held, high, lower, jnp.zeros((fill, total), F32)], axis=0
    ).astype(BF16)

    def body(c, carry):
        at = aligned(c * chunk, chunk)
        pick = jnp.where(iota((chunk, total), 0) + at == target, 1.0, 0.0).astype(BF16)
        out[pl.ds(at, chunk), :] = dot_nt(pick, data).astype(BF16)
        return carry

    lax.fori_loop(0, out.shape[0] // chunk, body, 0)


def forcing_body(dims, chunk, got, forcing, left, right):
    tracers, levels, rows = dims
    padded = left.shape[0] // rows

    def body(c, carry):
        at = aligned(c * chunk, chunk)
        part = got[pl.ds(at, chunk), :].astype(F32)
        lane = iota((chunk, LANES), 1).astype(F32)
        hit = part[:, levels + tracers + 1 : levels + tracers + 2] == lane
        for t in range(tracers):
            right[:, t * LANES : (t + 1) * LANES] = jnp.where(
                hit, part[:, levels + t : levels + t + 1], 0.0
            ).astype(BF16)
        turned = part.T
        high = turned[levels + tracers : levels + tracers + 1, :]
        sub = iota((rows, chunk), 0).astype(F32)
        mine = sub == high
        for k2 in range(padded // 2):
            two = []
            for k in (2 * k2, 2 * k2 + 1):
                two.append(jnp.where(mine, turned[k : k + 1, :], 0.0) if k < levels else jnp.zeros((rows, chunk), F32))
            left[2 * k2 * rows : (2 * k2 + 2) * rows, :] = jnp.concatenate(two, axis=0).astype(BF16)
        value = jnp.dot(left[...], right[...], preferred_element_type=F32)

        @pl.when(c == 0)
        def _():
            forcing[...] = value

        @pl.when(c > 0)
        def _():
            forcing[...] += value

        return carry

    lax.fori_loop(0, got.shape[0] // chunk, body, 0)


def lat_body(tracers, rows, offsets, matrix, *rest):
    *parts, out = rest
    size = tracers * rows
    total_rows = matrix.shape[0]
    bands = total_rows // rows
    lat = lax.axis_index("lat")
    depth = size + (2 * tracers + 7) // 8 * 8
    each = depth + 8
    width = each * len(parts)
    own = matrix[pl.ds(pl.multiple_of(lat * rows, rows), rows), :]
    own = jnp.concatenate([own] * tracers, axis=0)
    column = iota((1, width), 1) % each
    band = jnp.zeros((1, width), jnp.int32)
    for b, offset in enumerate(offsets):
        band = jnp.where(iota((1, width), 1) // each == b, lax.rem(lat + offset + bands, bands), band)
    in_band = jnp.where(column < size, column % rows, jnp.where(column < size + tracers, -1, rows))
    source = jnp.where(column < size + 2 * tracers, band * rows + in_band, -1)
    of_tracer = jnp.where(column < size, column // rows, (column - size) % tracers)
    hit = (iota((total_rows, width), 0) == source).astype(BF16)
    same = iota((size, width), 0) // rows == of_tracer
    weights = jnp.where(same, jnp.dot(own, hit, preferred_element_type=F32), 0.0).astype(BF16)
    patches = jnp.concatenate([p[p.shape[0] - each :, :] for p in parts], axis=0)
    total = jnp.dot(weights, patches, preferred_element_type=F32)
    ends = jnp.concatenate([p[p.shape[0] - 8 :, 0:each].astype(F32) for p in parts], axis=1).astype(BF16)
    ends = dot_nt(ends, weights)
    ends = jnp.concatenate([ends, jnp.zeros((8, LANES - size), F32)], axis=1)
    whole = jnp.concatenate([total, ends], axis=0).astype(BF16)
    out[...] = whole


def lon_body(matrix, *rest):
    *parts, out = rest
    count = len(parts)
    size = out.shape[0]
    lon = lax.axis_index("lon")
    ends = [p[size : size + 8, :].astype(F32)[:, 0:size] for p in parts]
    east = jnp.concatenate([ends[(s + 1) % count][1:2] for s in range(count)], axis=1)
    west = jnp.concatenate([ends[(s - 1) % count][0:1] for s in range(count)], axis=1)
    sides = spread_columns(east, west)
    total = jnp.zeros(out.shape, F32)
    for s, part in enumerate(parts):
        block = (part[0:size, :].astype(F32) + sides[s * size : (s + 1) * size, :]).astype(BF16)
        source = lax.rem(lon - s + count, count)
        own = matrix[:, pl.ds(pl.multiple_of(source * LANES, LANES), LANES)]
        total = total + dot_nt(block, own)
    out[...] = total


def ring(axis, step):
    count = lax.axis_size(axis)
    return [(i, (i + step) % count) for i in range(count)]


def exchange(up, down, to_west, to_east):
    south = lax.ppermute(up, "lat", ring("lat", 1))
    north = lax.ppermute(down, "lat", ring("lat", -1))
    east = lax.ppermute(to_west, "lon", ring("lon", -1))
    west = lax.ppermute(to_east, "lon", ring("lon", 1))
    return north, south, east, west


def window(
    adjoint_in,
    fractions,
    profiles,
    kernel,
    obs_weights,
    obs_resid,
    obs_cols,
    obs_owner,
    obs_count,
    lat_matrix,
    lon_matrix,
):
    dims = tracers, levels, rows = adjoint_in.shape[:3]
    assert adjoint_in.shape[3] == LANES
    padded = (levels + 1) // 2 * 2
    count = tracers * levels
    cells = count * rows
    wide = tracers * LANES
    devices = lax.axis_size(BOTH)
    state = jax.ShapeDtypeStruct((cells, LANES), F32)
    row_edge = jax.ShapeDtypeStruct((count, LANES), BF16)
    side_edge = jax.ShapeDtypeStruct((1, cells), F32)
    edges = [row_edge, row_edge, side_edge, side_edge]
    long_row = jax.ShapeDtypeStruct((count + 16, LANES), BF16)
    long_side = jax.ShapeDtypeStruct((1, (cells + LANES - 1) // LANES * LANES + LANES), F32)
    long_edges = [long_row, long_row, long_side, long_side]
    level_zero = pl.BlockSpec((1, 4, 1, rows, LANES), lambda i: (0, 0, 0, 0, 0))
    kron_type = jax.ShapeDtypeStruct((padded * rows, padded * rows), BF16)
    surface_type = jax.ShapeDtypeStruct((tracers * rows, LANES), F32)
    low_scr = pltpu.VMEM((padded * rows, wide), BF16)
    mix_scr = pltpu.VMEM((padded * rows, wide), F32)
    halo_scr = [
        pltpu.VMEM(((count + 7) // 8 * 8, LANES), F32),
        pltpu.VMEM(((count + 7) // 8 * 8, LANES), F32),
        pltpu.VMEM((cells, LANES), F32),
    ]

    def spec(leaf):
        return full(leaf.shape)

    mixed, kron, *out = pl.pallas_call(
        functools.partial(first_body, dims),
        grid=(1,),
        out_shape=[state, kron_type] + long_edges,
        in_specs=[full(kernel.shape), full(profiles.shape), spec(state), level_zero],
        out_specs=[pl.BlockSpec(memory_space=pltpu.HBM)] * 2 + [spec(s) for s in long_edges],
        scratch_shapes=[
            low_scr,
            mix_scr,
            pltpu.VMEM(state.shape, state.dtype),
            pltpu.VMEM(kron_type.shape, kron_type.dtype),
            pltpu.SemaphoreType.DMA,
            pltpu.SemaphoreType.DMA,
        ],
        compiler_params=params(60 << 20),
        name="first",
    )(kernel, profiles, adjoint_in.reshape(cells, LANES), fractions)
    halo = first_halo = exchange(*out)
    obs_count, _ = lax.optimization_barrier((obs_count, out[2]))

    blocks = obs_count.shape[0]
    slots = obs_cols.shape[0] // blocks
    rows_out = devices * CAPACITY * slots
    packed = pl.pallas_call(
        functools.partial(pack_body, (devices, blocks, slots, levels, tracers, 8 * CAPACITY * slots)),
        grid=(1,),
        out_shape=jax.ShapeDtypeStruct((rows_out, LANES), BF16),
        in_specs=[
            full((1, blocks)),
            full((1, blocks)),
            full((1, blocks * slots)),
            full(obs_weights.shape),
            full(obs_resid.shape),
        ],
        out_specs=full((rows_out, LANES)),
        compiler_params=params(60 << 20),
        name="pack",
    )(
        obs_owner.reshape(1, blocks),
        obs_count.reshape(1, blocks),
        obs_cols.reshape(1, blocks * slots),
        obs_weights,
        obs_resid,
    )
    got = lax.all_to_all(
        packed.reshape(devices, CAPACITY * slots, LANES), BOTH, split_axis=0, concat_axis=0, tiled=True
    )
    chunk = min(rows_out, 1536)
    forcing = pl.pallas_call(
        functools.partial(forcing_body, dims, chunk),
        out_shape=jax.ShapeDtypeStruct((padded * rows, wide), F32),
        scratch_shapes=[pltpu.VMEM((padded * rows, chunk), BF16), pltpu.VMEM((chunk, wide), BF16)],
        compiler_params=params(),
        name="forcing",
    )(got.reshape(rows_out, LANES))

    surface = jnp.zeros(surface_type.shape, F32)
    lon_count = lax.axis_size("lon")
    patch_rows = (tracers * (rows + 2) + 7) // 8 * 8
    patch_type = jax.ShapeDtypeStruct((patch_rows + 8, LANES), BF16)
    tall = jax.ShapeDtypeStruct(((count + 15) // 16 * 16 + patch_type.shape[0], LANES), BF16)
    for step_index in range(STEPS - 1, 0, -1):
        last = step_index == 1
        frac_spec = pl.BlockSpec((1,) + fractions.shape[1:], lambda i, n=step_index: (n, 0, 0, 0, 0))
        halo_types = long_edges if step_index == STEPS - 1 else edges
        outs = [tall, tall, side_edge, side_edge] if last else edges
        ins = [mixed, *halo, fractions, profiles, kron, surface]
        in_specs = [spec(state)] + [spec(h) for h in halo_types]
        in_specs += [frac_spec, full(profiles.shape), spec(kron_type), spec(surface_type)]
        result = surface_type
        if last:
            ins += [fractions, forcing, *first_halo]
            in_specs += [level_zero, pl.BlockSpec((rows, wide), lambda i: (0, 0))] + [spec(h) for h in long_edges]
            result = patch_type
        mixed, *out, surface = pl.pallas_call(
            functools.partial(step_body, dims, last),
            grid=(1,),
            out_shape=[state] + outs + [result],
            in_specs=in_specs,
            out_specs=[spec(s) for s in [state] + outs + [result]],
            scratch_shapes=halo_scr + [pltpu.VMEM((cells, LANES), F32), low_scr, mix_scr],
            compiler_params=params(),
            name="step",
        )(*ins)
        halo = exchange(*out)

    lat_count = lax.axis_size("lat")
    parts = [surface, halo[1], halo[0]]
    offsets = [0, -1, 1]
    for shift in range(2, lat_count - 1):
        parts.append(lax.ppermute(surface, "lat", ring("lat", shift)))
        offsets.append(-shift)
    bands = pl.pallas_call(
        functools.partial(lat_body, tracers, rows, offsets),
        out_shape=jax.ShapeDtypeStruct((tracers * rows + 8, LANES), BF16),
        compiler_params=params(),
        name="lat_smooth",
    )(lat_matrix, *parts)
    shifts = [lax.ppermute(bands, "lon", ring("lon", shift)) for shift in range(1, lon_count)]
    frac_spec = pl.BlockSpec((1,) + fractions.shape[1:], lambda i: (0, 0, 0, 0, 0))
    adjoint = pl.pallas_call(
        functools.partial(last_body, dims),
        grid=(1,),
        out_shape=state,
        in_specs=[spec(state), spec(tall), spec(tall), spec(side_edge), spec(side_edge)]
        + [frac_spec, full(forcing.shape)],
        out_specs=spec(state),
        scratch_shapes=halo_scr,
        compiler_params=params(),
        name="last",
    )(mixed, *halo, fractions, forcing)
    smoothed = pl.pallas_call(
        lon_body,
        out_shape=surface_type,
        compiler_params=params(),
        name="lon_smooth",
    )(lon_matrix, bands, *shifts)
    return adjoint.reshape(adjoint_in.shape), smoothed.reshape(tracers, rows, LANES)


def solution(mesh):
    placed = (
        P(None, None, "lat", "lon"),
        P(None, None, None, "lat", "lon"),
        P(None, None, "lat", "lon"),
        P(),
        P(None, BOTH),
        P(None, BOTH),
        P(BOTH),
        P(BOTH, None),
        P(BOTH),
        P(),
        P("lon", None),
    )
    return jax.shard_map(
        window,
        mesh=mesh,
        in_specs=placed,
        out_specs=(P(None, None, "lat", "lon"), P(None, "lat", "lon")),
        check_vma=False,
    )
```

```python
import functools

import jax
import jax.numpy as jnp
from jax import lax
from jax.experimental import pallas as pl
from jax.experimental.pallas import tpu as pltpu
from jax.sharding import PartitionSpec as P

STEPS = 4
CAPACITY = 6
F32 = jnp.float32
BF16 = jnp.bfloat16
BOTH = ("lat", "lon")
LANES = 128


def aligned(value, by):
    return value if isinstance(value, int) else pl.multiple_of(value, by)


def iota(shape, dim):
    return lax.broadcasted_iota(jnp.int32, shape, dim)


def dot_nt(a, b):
    return lax.dot_general(a, b, (((1,), (1,)), ((), ())), preferred_element_type=F32)


def dot_tn(a, b):
    return lax.dot_general(a, b, (((0,), (0,)), ((), ())), preferred_element_type=F32)


def full(shape):
    return pl.BlockSpec(shape, lambda i: (0,) * len(shape))


def params(limit=24 << 20):
    return pltpu.CompilerParams(vmem_limit_bytes=limit)


def expand_kernel(kernel, levels, padded, rows):
    size = padded * rows
    spread = (iota((size, levels), 0) // rows == iota((size, levels), 1)).astype(BF16)
    half = dot_nt(spread, kernel).astype(BF16)
    whole = dot_nt(half, spread)
    same = iota((size, size), 0) % rows == iota((size, size), 1) % rows
    return jnp.where(same, whole, 0.0).astype(BF16)


def convect(dims, adj, low, mix, kron, profiles, mixed):
    tracers, levels, rows = dims
    mix[...] = jnp.dot(kron[...], low[...], preferred_element_type=F32)

    def body(k2, ks):
        for k in ks:
            entrain = profiles[0, k].astype(F32)
            start = aligned(k * rows, rows)
            for t in range(tracers):
                at = aligned((t * levels + k) * rows, rows)
                mixed[pl.ds(at, rows), :] = adj[pl.ds(at, rows), :] + entrain * mix[
                    pl.ds(start, rows), t * LANES : (t + 1) * LANES
                ]

    over_levels(levels, body)


def end_columns(rows_2d):
    lane = iota((8, LANES), 1)
    sub = iota((8, LANES), 0)
    pick = ((sub == 0) & (lane == 0)) | ((sub == 1) & (lane == LANES - 1))
    return dot_nt(pick.astype(BF16), rows_2d.astype(BF16))


def spread_columns(first, last):
    lane = iota((8, LANES), 1)
    sub = iota((8, first.shape[1]), 0)
    got = jnp.where(sub == 0, last, jnp.where(sub == 1, first, 0.0)).astype(BF16)
    sub = iota((8, LANES), 0)
    place = (((sub == 0) & (lane == LANES - 1)) | ((sub == 1) & (lane == 0))).astype(BF16)
    return dot_tn(got, place)


def send_edges(dims, mixed, up, down, west, east):
    tracers, levels, rows = dims
    count = tracers * levels
    lat = lax.axis_index("lat")
    last = lax.axis_size("lat") - 1
    first_row = mixed[pl.ds(0, count, stride=rows), :]
    last_row = mixed[pl.ds(rows - 1, count, stride=rows), :]
    up[0:count, :] = jnp.where(lat < last, last_row, 0.0).astype(BF16)
    down[0:count, :] = jnp.where(lat > 0, first_row, 0.0).astype(BF16)
    sides = end_columns(mixed[...])
    west[:, 0 : count * rows] = sides[0:1]
    east[:, 0 : count * rows] = sides[1:2]


def store_low(low, k2, rows, t, parts):
    low[pl.ds(aligned(k2 * 2 * rows, 2 * rows), 2 * rows), t * LANES : (t + 1) * LANES] = jnp.concatenate(
        parts, axis=0
    ).astype(BF16)


def over_levels(levels, body):
    for k2 in range(levels // 2):
        body(k2, (2 * k2, 2 * k2 + 1))
    if levels % 2:
        body(levels // 2, (levels - 1,))


def first_body(dims, kernel, profiles, adjoint, fraction, mixed_out, kron_out, up, down, west, east, *rest):
    low, mix, mixed, kron, mixed_sem, kron_sem = rest
    tracers, levels, rows = dims
    kron[...] = expand_kernel(kernel[...], levels, low.shape[0] // rows, rows)
    kron_copy = pltpu.make_async_copy(kron, kron_out, kron_sem)
    kron_copy.start()

    def body(k2, ks):
        detrains = [profiles[1, k].astype(F32) for k in ks]
        for t in range(tracers):
            parts = [
                d * adjoint[pl.ds(aligned((t * levels + k) * rows, rows), rows), :] for d, k in zip(detrains, ks)
            ]
            store_low(low, k2, rows, t, parts if len(parts) == 2 else parts + [jnp.zeros_like(parts[0])])

    over_levels(levels, body)
    convect(dims, adjoint, low, mix, kron, profiles, mixed)
    mixed_copy = pltpu.make_async_copy(mixed, mixed_out, mixed_sem)
    mixed_copy.start()
    send_edges(dims, mixed, up, down, west, east)
    count = tracers * levels
    lat = lax.axis_index("lat")
    last = lax.axis_size("lat") - 1
    f = [fraction[0, d, 0].astype(F32) for d in range(4)]
    pad = jnp.zeros((up.shape[0] - count - 1, LANES), F32)
    up[count:, :] = jnp.concatenate([jnp.where(lat < last, f[2][rows - 1 :], 0.0), pad], axis=0).astype(BF16)
    down[count:, :] = jnp.concatenate([jnp.where(lat > 0, f[3][:1], 0.0), pad], axis=0).astype(BF16)
    at = (count * rows + LANES - 1) // LANES * LANES
    west[:, at : at + tracers * rows] = end_columns(jnp.concatenate([f[1]] * tracers, axis=0))[0:1]
    east[:, at : at + tracers * rows] = end_columns(jnp.concatenate([f[0]] * tracers, axis=0))[1:2]
    kron_copy.wait()
    mixed_copy.wait()


def unpack_halo(dims, north, south, east, west, north_scr, south_scr, sides):
    tracers, levels, rows = dims
    count = tracers * levels
    north_scr[0:count, :] = north[0:count, :].astype(F32)
    south_scr[0:count, :] = south[0:count, :].astype(F32)
    sides[...] = spread_columns(west[:, 0 : count * rows], east[:, 0 : count * rows])


def transport(dims, k, fraction, mixed, north_scr, south_scr, sides):
    tracers, levels, rows = dims
    f = [fraction[0, d, k].astype(F32) for d in range(4)]
    remain = 1.0 - f[0] - f[1] - f[2] - f[3]
    lane = iota((rows, LANES), 1)
    sub = iota((rows, LANES), 0)
    out = []
    for t in range(tracers):
        index = t * levels + k
        at = pl.ds(aligned(index * rows, rows), rows)
        m = mixed[at, :]
        side = sides[at, :]
        east = jnp.where(lane == LANES - 1, side, pltpu.roll(m, LANES - 1, 1))
        west = jnp.where(lane == 0, side, pltpu.roll(m, 1, 1))
        north = jnp.where(
            sub == rows - 1,
            jnp.broadcast_to(north_scr[pl.ds(index, 1), :], (rows, LANES)),
            pltpu.roll(m, rows - 1, 0),
        )
        south = jnp.where(
            sub == 0, jnp.broadcast_to(south_scr[pl.ds(index, 1), :], (rows, LANES)), pltpu.roll(m, 1, 0)
        )
        out.append((at, remain * m + f[0] * east + f[1] * west + f[2] * north + f[3] * south))
    return out


def step_body(dims, opening, last, mixed, north, south, east, west, fraction, profiles, kron, *rest):
    surface = None
    if not opening:
        surface, *rest = rest
    if last:
        extra, rest = rest[:6], rest[6:]
    new_mixed, up, down, to_west, to_east, new_surface, north_scr, south_scr, sides, adj, low, mix = rest
    tracers, levels, rows = dims
    unpack_halo(dims, north, south, east, west, north_scr, south_scr, sides)

    def body(k2, ks):
        parts = [[] for _ in range(tracers)]
        for k in ks:
            detrain = profiles[1, k].astype(F32)
            for t, (at, value) in enumerate(transport(dims, k, fraction, mixed, north_scr, south_scr, sides)):
                adj[at, :] = value
                parts[t].append(detrain * value)
        for t in range(tracers):
            two = parts[t] if len(ks) == 2 else parts[t] + [jnp.zeros_like(parts[t][0])]
            store_low(low, k2, rows, t, two)

    over_levels(levels, body)
    convect(dims, adj, low, mix, kron, profiles, new_mixed)
    send_edges(dims, new_mixed, up, down, to_west, to_east)
    total = [adj[t * levels * rows : t * levels * rows + rows, :] for t in range(tracers)]
    if surface is not None:
        total = [surface[t * rows : (t + 1) * rows, :] + total[t] for t in range(tracers)]
    if last:
        patch(dims, new_mixed, total, *extra, new_surface)
        at = up.shape[0] - new_surface.shape[0]
        up[at:, :] = new_surface[...]
        down[at:, :] = new_surface[...]
    else:
        new_surface[...] = jnp.concatenate(total, axis=0)


def patch(dims, mixed, total, fraction, forcing, north, south, east, west, out):
    tracers, levels, rows = dims
    count = tracers * levels
    f = [fraction[0, d, 0].astype(F32) for d in range(4)]
    remain = 1.0 - f[0] - f[1] - f[2] - f[3]
    lane = iota((rows, LANES), 1)
    sub = iota((rows, LANES), 0)
    below = south[count : count + 8, :].astype(F32)[0:1]
    above = north[count : count + 8, :].astype(F32)[0:1]
    tile, under, over = [], [], []
    for t in range(tracers):
        m = mixed[t * levels * rows : t * levels * rows + rows, :]
        value = remain * m
        value = value + f[0] * jnp.where(lane == LANES - 1, 0.0, pltpu.roll(m, LANES - 1, 1))
        value = value + f[1] * jnp.where(lane == 0, 0.0, pltpu.roll(m, 1, 1))
        value = value + f[2] * jnp.where(sub == rows - 1, 0.0, pltpu.roll(m, rows - 1, 0))
        value = value + f[3] * jnp.where(sub == 0, 0.0, pltpu.roll(m, 1, 0))
        tile.append(total[t] + value + forcing[0:rows, t * LANES : (t + 1) * LANES])
        under.append(below * m[0:1])
        over.append(above * m[rows - 1 : rows])
    tops = jnp.concatenate([mixed[t * levels * rows : t * levels * rows + rows, :] for t in range(tracers)], axis=0)
    columns = end_columns(tops)
    at = (count * rows + LANES - 1) // LANES * LANES
    size = tracers * rows
    to_west = columns[0:1] * west[:, at : at + size]
    to_east = columns[1:2] * east[:, at : at + size]
    ends = jnp.concatenate([to_west, to_east, jnp.zeros((6, size), F32)], axis=0)
    ends = jnp.concatenate([ends, jnp.zeros((8, LANES - size), F32)], axis=1)
    short = (-2 * tracers) % 8
    filler = [jnp.zeros((short, LANES), F32)] if short else []
    whole = jnp.concatenate(tile + under + over + filler + [ends], axis=0)
    out[...] = whole.astype(BF16)


def last_body(dims, mixed, north, south, east, west, fraction, forcing, *rest):
    adjoint, north_scr, south_scr, sides = rest
    _, levels, rows = dims
    unpack_halo(dims, north, south, east, west, north_scr, south_scr, sides)

    def body(k2, ks):
        for k in ks:
            start = aligned(k * rows, rows)
            for t, (at, value) in enumerate(transport(dims, k, fraction, mixed, north_scr, south_scr, sides)):
                adjoint[at, :] = value + forcing[pl.ds(start, rows), t * LANES : (t + 1) * LANES]

    over_levels(levels, body)


def pack_body(sizes, owner, count, cols, weights, resid, out):
    _, blocks, slots, levels, tracers, chunk = sizes
    own = owner[...].astype(F32)
    wide = jnp.broadcast_to(own, (blocks, blocks))
    below = iota((blocks, blocks), 0)
    along = iota((blocks, blocks), 1)
    own_col = jnp.sum(jnp.where(below == along, wide, 0.0), axis=1, keepdims=True)
    earlier = jnp.where((own_col == wide) & (below < along), 1.0, 0.0)
    rank = jnp.sum(earlier, axis=0, keepdims=True)
    table = jnp.concatenate(
        [own, rank, count[...].astype(F32), jnp.zeros((5, blocks), F32)], axis=0
    ).astype(BF16)
    total = blocks * slots
    spread = (iota((blocks, total), 1) // slots == iota((blocks, total), 0)).astype(BF16)
    each = jnp.dot(table, spread, preferred_element_type=F32)
    slot = iota((1, total), 1) % slots
    target = (each[0:1].astype(jnp.int32) * CAPACITY + each[1:2].astype(jnp.int32)) * slots + slot
    valid = slot < each[2:3].astype(jnp.int32)
    held = jnp.where(valid, resid[...].astype(F32), 0.0)
    place = cols[...]
    high = (place // LANES).astype(F32)
    lower = (place % LANES).astype(F32)
    fill = LANES - levels - tracers - 2
    data = jnp.concatenate(
        [weights[...].astype(F32), held, high, lower, jnp.zeros((fill, total), F32)], axis=0
    ).astype(BF16)

    def body(c, carry):
        at = aligned(c * chunk, chunk)
        pick = jnp.where(iota((chunk, total), 0) + at == target, 1.0, 0.0).astype(BF16)
        out[pl.ds(at, chunk), :] = dot_nt(pick, data).astype(BF16)
        return carry

    lax.fori_loop(0, out.shape[0] // chunk, body, 0)


def forcing_body(dims, chunk, got, forcing, left, right):
    tracers, levels, rows = dims
    padded = left.shape[0] // rows

    def body(c, carry):
        at = aligned(c * chunk, chunk)
        part = got[pl.ds(at, chunk), :].astype(F32)
        lane = iota((chunk, LANES), 1).astype(F32)
        hit = part[:, levels + tracers + 1 : levels + tracers + 2] == lane
        for t in range(tracers):
            right[:, t * LANES : (t + 1) * LANES] = jnp.where(
                hit, part[:, levels + t : levels + t + 1], 0.0
            ).astype(BF16)
        turned = part.T
        high = turned[levels + tracers : levels + tracers + 1, :]
        sub = iota((rows, chunk), 0).astype(F32)
        mine = sub == high
        for k2 in range(padded // 2):
            two = []
            for k in (2 * k2, 2 * k2 + 1):
                two.append(jnp.where(mine, turned[k : k + 1, :], 0.0) if k < levels else jnp.zeros((rows, chunk), F32))
            left[2 * k2 * rows : (2 * k2 + 2) * rows, :] = jnp.concatenate(two, axis=0).astype(BF16)
        value = jnp.dot(left[...], right[...], preferred_element_type=F32)

        @pl.when(c == 0)
        def _():
            forcing[...] = value

        @pl.when(c > 0)
        def _():
            forcing[...] += value

        return carry

    lax.fori_loop(0, got.shape[0] // chunk, body, 0)


def lat_body(tracers, rows, offsets, matrix, *rest):
    *parts, out = rest
    size = tracers * rows
    total_rows = matrix.shape[0]
    bands = total_rows // rows
    lat = lax.axis_index("lat")
    depth = size + (2 * tracers + 7) // 8 * 8
    each = depth + 8
    width = each * len(parts)
    own = matrix[pl.ds(pl.multiple_of(lat * rows, rows), rows), :]
    own = jnp.concatenate([own] * tracers, axis=0)
    column = iota((1, width), 1) % each
    band = jnp.zeros((1, width), jnp.int32)
    for b, offset in enumerate(offsets):
        band = jnp.where(iota((1, width), 1) // each == b, lax.rem(lat + offset + bands, bands), band)
    in_band = jnp.where(column < size, column % rows, jnp.where(column < size + tracers, -1, rows))
    source = jnp.where(column < size + 2 * tracers, band * rows + in_band, -1)
    of_tracer = jnp.where(column < size, column // rows, (column - size) % tracers)
    hit = (iota((total_rows, width), 0) == source).astype(BF16)
    same = iota((size, width), 0) // rows == of_tracer
    weights = jnp.where(same, jnp.dot(own, hit, preferred_element_type=F32), 0.0).astype(BF16)
    patches = jnp.concatenate([p[p.shape[0] - each :, :] for p in parts], axis=0)
    total = jnp.dot(weights, patches, preferred_element_type=F32)
    ends = jnp.concatenate([p[p.shape[0] - 8 :, 0:each].astype(F32) for p in parts], axis=1).astype(BF16)
    ends = dot_nt(ends, weights)
    ends = jnp.concatenate([ends, jnp.zeros((8, LANES - size), F32)], axis=1)
    out[...] = jnp.concatenate([total, ends], axis=0)


def pair_body(own, other, out):
    half = own.shape[0]
    first_core = lax.axis_index("lon") % 2 == 0
    out[0:half, :] = jnp.where(first_core, own[...], other[...])
    out[half:, :] = jnp.where(first_core, other[...], own[...])


def lon_body(matrix, *rest):
    *pairs, out = rest
    half = pairs[0].shape[0] // 2
    parts = [p[at : at + half, :] for p in pairs for at in (half, 0)]
    count = len(parts)
    size = out.shape[0]
    lon = lax.axis_index("lon") // 2 * 2 + 1
    ends = [p[size : size + 8, :].astype(F32)[:, 0:size] for p in parts]
    east = jnp.concatenate([ends[(s + 1) % count][1:2] for s in range(count)], axis=1)
    west = jnp.concatenate([ends[(s - 1) % count][0:1] for s in range(count)], axis=1)
    sides = spread_columns(east, west)
    total = jnp.zeros(out.shape, F32)
    for s, part in enumerate(parts):
        block = (part[0:size, :].astype(F32) + sides[s * size : (s + 1) * size, :]).astype(BF16)
        source = lax.rem(lon - s + count, count)
        own = matrix[:, pl.ds(pl.multiple_of(source * LANES, LANES), LANES)]
        total = total + dot_nt(block, own)
    out[...] = total


def ring(axis, step):
    count = lax.axis_size(axis)
    return [(i, (i + step) % count) for i in range(count)]


def exchange(up, down, to_west, to_east):
    south = lax.ppermute(up, "lat", ring("lat", 1))
    north = lax.ppermute(down, "lat", ring("lat", -1))
    east = lax.ppermute(to_west, "lon", ring("lon", -1))
    west = lax.ppermute(to_east, "lon", ring("lon", 1))
    return north, south, east, west


def window(
    adjoint_in,
    fractions,
    profiles,
    kernel,
    obs_weights,
    obs_resid,
    obs_cols,
    obs_owner,
    obs_count,
    lat_matrix,
    lon_matrix,
):
    dims = tracers, levels, rows = adjoint_in.shape[:3]
    assert adjoint_in.shape[3] == LANES
    padded = (levels + 1) // 2 * 2
    count = tracers * levels
    cells = count * rows
    wide = tracers * LANES
    devices = lax.axis_size(BOTH)
    state = jax.ShapeDtypeStruct((cells, LANES), F32)
    row_edge = jax.ShapeDtypeStruct((count, LANES), BF16)
    side_edge = jax.ShapeDtypeStruct((1, cells), F32)
    edges = [row_edge, row_edge, side_edge, side_edge]
    long_row = jax.ShapeDtypeStruct((count + 16, LANES), BF16)
    long_side = jax.ShapeDtypeStruct((1, (cells + LANES - 1) // LANES * LANES + LANES), F32)
    long_edges = [long_row, long_row, long_side, long_side]
    level_zero = pl.BlockSpec((1, 4, 1, rows, LANES), lambda i: (0, 0, 0, 0, 0))
    kron_type = jax.ShapeDtypeStruct((padded * rows, padded * rows), BF16)
    surface_type = jax.ShapeDtypeStruct((tracers * rows, LANES), F32)
    low_scr = pltpu.VMEM((padded * rows, wide), BF16)
    mix_scr = pltpu.VMEM((padded * rows, wide), F32)
    halo_scr = [
        pltpu.VMEM(((count + 7) // 8 * 8, LANES), F32),
        pltpu.VMEM(((count + 7) // 8 * 8, LANES), F32),
        pltpu.VMEM((cells, LANES), F32),
    ]

    def spec(leaf):
        return full(leaf.shape)

    mixed, kron, *out = pl.pallas_call(
        functools.partial(first_body, dims),
        grid=(1,),
        out_shape=[state, kron_type] + long_edges,
        in_specs=[full(kernel.shape), full(profiles.shape), spec(state), level_zero],
        out_specs=[pl.BlockSpec(memory_space=pltpu.HBM)] * 2 + [spec(s) for s in long_edges],
        scratch_shapes=[
            low_scr,
            mix_scr,
            pltpu.VMEM(state.shape, state.dtype),
            pltpu.VMEM(kron_type.shape, kron_type.dtype),
            pltpu.SemaphoreType.DMA,
            pltpu.SemaphoreType.DMA,
        ],
        compiler_params=params(60 << 20),
        name="first",
    )(kernel, profiles, adjoint_in.reshape(cells, LANES), fractions)
    halo = first_halo = exchange(*out)
    obs_count, _ = lax.optimization_barrier((obs_count, out[2]))

    blocks = obs_count.shape[0]
    slots = obs_cols.shape[0] // blocks
    rows_out = devices * CAPACITY * slots
    packed = pl.pallas_call(
        functools.partial(pack_body, (devices, blocks, slots, levels, tracers, 8 * CAPACITY * slots)),
        grid=(1,),
        out_shape=jax.ShapeDtypeStruct((rows_out, LANES), BF16),
        in_specs=[
            full((1, blocks)),
            full((1, blocks)),
            full((1, blocks * slots)),
            full(obs_weights.shape),
            full(obs_resid.shape),
        ],
        out_specs=full((rows_out, LANES)),
        compiler_params=params(),
        name="pack",
    )(
        obs_owner.reshape(1, blocks),
        obs_count.reshape(1, blocks),
        obs_cols.reshape(1, blocks * slots),
        obs_weights,
        obs_resid,
    )
    got = lax.all_to_all(
        packed.reshape(devices, CAPACITY * slots, LANES), BOTH, split_axis=0, concat_axis=0, tiled=True
    )
    chunk = min(rows_out, 1536)
    forcing = pl.pallas_call(
        functools.partial(forcing_body, dims, chunk),
        out_shape=jax.ShapeDtypeStruct((padded * rows, wide), F32),
        scratch_shapes=[pltpu.VMEM((padded * rows, chunk), BF16), pltpu.VMEM((chunk, wide), BF16)],
        compiler_params=params(),
        name="forcing",
    )(got.reshape(rows_out, LANES))

    lon_count = lax.axis_size("lon")
    patch_rows = (tracers * (rows + 2) + 7) // 8 * 8
    patch_type = jax.ShapeDtypeStruct((patch_rows + 8, LANES), BF16)
    tall = jax.ShapeDtypeStruct(((count + 15) // 16 * 16 + patch_type.shape[0], LANES), BF16)
    for step_index in range(STEPS - 1, 0, -1):
        last = step_index == 1
        frac_spec = pl.BlockSpec((1,) + fractions.shape[1:], lambda i, n=step_index: (n, 0, 0, 0, 0))
        halo_types = long_edges if step_index == STEPS - 1 else edges
        outs = [tall, tall, side_edge, side_edge] if last else edges
        opening = step_index == STEPS - 1
        ins = [mixed, *halo, fractions, profiles, kron]
        in_specs = [spec(state)] + [spec(h) for h in halo_types]
        in_specs += [frac_spec, full(profiles.shape), spec(kron_type)]
        if not opening:
            ins.append(surface)
            in_specs.append(spec(surface_type))
        result = surface_type
        if last:
            ins += [fractions, forcing, *first_halo]
            in_specs += [level_zero, pl.BlockSpec((rows, wide), lambda i: (0, 0))] + [spec(h) for h in long_edges]
            result = patch_type
        mixed, *out, surface = pl.pallas_call(
            functools.partial(step_body, dims, opening, last),
            grid=(1,),
            out_shape=[state] + outs + [result],
            in_specs=in_specs,
            out_specs=[spec(s) for s in [state] + outs + [result]],
            scratch_shapes=halo_scr + [pltpu.VMEM((cells, LANES), F32), low_scr, mix_scr],
            compiler_params=params(),
            name="step",
        )(*ins)
        halo = exchange(*out)

    lat_count = lax.axis_size("lat")
    parts = [surface, halo[1], halo[0]]
    offsets = [0, -1, 1]
    for shift in range(2, lat_count - 1):
        parts.append(lax.ppermute(surface, "lat", ring("lat", shift)))
        offsets.append(-shift)
    bands = pl.pallas_call(
        functools.partial(lat_body, tracers, rows, offsets),
        out_shape=jax.ShapeDtypeStruct((tracers * rows + 8, LANES), F32),
        compiler_params=params(),
        name="lat_smooth",
    )(lat_matrix, *parts)
    other = lax.ppermute(bands, "lon", [(i, i ^ 1) for i in range(lon_count)])
    pair = pl.pallas_call(
        pair_body,
        out_shape=jax.ShapeDtypeStruct((2 * bands.shape[0], LANES), F32),
        compiler_params=params(),
        name="pair",
    )(bands, other)
    shifts = [lax.ppermute(pair, "lon", ring("lon", shift)) for shift in range(2, lon_count, 2)]
    frac_spec = pl.BlockSpec((1,) + fractions.shape[1:], lambda i: (0, 0, 0, 0, 0))
    adjoint = pl.pallas_call(
        functools.partial(last_body, dims),
        grid=(1,),
        out_shape=state,
        in_specs=[spec(state), spec(tall), spec(tall), spec(side_edge), spec(side_edge)]
        + [frac_spec, full(forcing.shape)],
        out_specs=spec(state),
        scratch_shapes=halo_scr,
        compiler_params=params(),
        name="last",
    )(mixed, *halo, fractions, forcing)
    smoothed = pl.pallas_call(
        lon_body,
        out_shape=surface_type,
        compiler_params=params(),
        name="lon_smooth",
    )(lon_matrix, pair, *shifts)
    return adjoint.reshape(adjoint_in.shape), smoothed.reshape(tracers, rows, LANES)


def solution(mesh):
    placed = (
        P(None, None, "lat", "lon"),
        P(None, None, None, "lat", "lon"),
        P(None, None, "lat", "lon"),
        P(),
        P(None, BOTH),
        P(None, BOTH),
        P(BOTH),
        P(BOTH, None),
        P(BOTH),
        P(),
        P("lon", None),
    )
    return jax.shard_map(
        window,
        mesh=mesh,
        in_specs=placed,
        out_specs=(P(None, None, "lat", "lon"), P(None, "lat", "lon")),
        check_vma=False,
    )
```

```python
import functools

import jax
import jax.numpy as jnp
from jax import lax
from jax.experimental import pallas as pl
from jax.experimental.pallas import tpu as pltpu
from jax.sharding import PartitionSpec as P

STEPS = 4
CAPACITY = 6
F32 = jnp.float32
BF16 = jnp.bfloat16
BOTH = ("lat", "lon")
LANES = 128


def aligned(value, by):
    return value if isinstance(value, int) else pl.multiple_of(value, by)


def iota(shape, dim):
    return lax.broadcasted_iota(jnp.int32, shape, dim)


def dot_nt(a, b):
    return lax.dot_general(a, b, (((1,), (1,)), ((), ())), preferred_element_type=F32)


def dot_tn(a, b):
    return lax.dot_general(a, b, (((0,), (0,)), ((), ())), preferred_element_type=F32)


def full(shape):
    return pl.BlockSpec(shape, lambda i: (0,) * len(shape))


def params(limit=24 << 20):
    return pltpu.CompilerParams(vmem_limit_bytes=limit)


def expand_kernel(kernel, levels, padded, rows):
    size = padded * rows
    spread = (iota((size, levels), 0) // rows == iota((size, levels), 1)).astype(BF16)
    half = dot_nt(spread, kernel).astype(BF16)
    whole = dot_nt(half, spread)
    same = iota((size, size), 0) % rows == iota((size, size), 1) % rows
    return jnp.where(same, whole, 0.0).astype(BF16)


def convect(dims, adj, low, mix, kron, profiles, mixed):
    tracers, levels, rows = dims
    mix[...] = jnp.dot(kron[...], low[...], preferred_element_type=F32)

    def body(k2, ks):
        for k in ks:
            entrain = profiles[0, k].astype(F32)
            start = aligned(k * rows, rows)
            for t in range(tracers):
                at = aligned((t * levels + k) * rows, rows)
                mixed[pl.ds(at, rows), :] = adj[pl.ds(at, rows), :] + entrain * mix[
                    pl.ds(start, rows), t * LANES : (t + 1) * LANES
                ]

    over_levels(levels, body)


def end_columns(rows_2d):
    lane = iota((8, LANES), 1)
    sub = iota((8, LANES), 0)
    pick = ((sub == 0) & (lane == 0)) | ((sub == 1) & (lane == LANES - 1))
    return dot_nt(pick.astype(BF16), rows_2d.astype(BF16))


def spread_columns(first, last):
    lane = iota((8, LANES), 1)
    sub = iota((8, first.shape[1]), 0)
    got = jnp.where(sub == 0, last, jnp.where(sub == 1, first, 0.0)).astype(BF16)
    sub = iota((8, LANES), 0)
    place = (((sub == 0) & (lane == LANES - 1)) | ((sub == 1) & (lane == 0))).astype(BF16)
    return dot_tn(got, place)


def send_edges(dims, mixed, up, down, west, east):
    tracers, levels, rows = dims
    count = tracers * levels
    lat = lax.axis_index("lat")
    last = lax.axis_size("lat") - 1
    first_row = mixed[pl.ds(0, count, stride=rows), :]
    last_row = mixed[pl.ds(rows - 1, count, stride=rows), :]
    up[0:count, :] = jnp.where(lat < last, last_row, 0.0).astype(BF16)
    down[0:count, :] = jnp.where(lat > 0, first_row, 0.0).astype(BF16)
    sides = end_columns(mixed[...])
    west[:, 0 : count * rows] = sides[0:1]
    east[:, 0 : count * rows] = sides[1:2]


def store_low(low, k2, rows, t, parts):
    low[pl.ds(aligned(k2 * 2 * rows, 2 * rows), 2 * rows), t * LANES : (t + 1) * LANES] = jnp.concatenate(
        parts, axis=0
    ).astype(BF16)


def over_levels(levels, body):
    for k2 in range(levels // 2):
        body(k2, (2 * k2, 2 * k2 + 1))
    if levels % 2:
        body(levels // 2, (levels - 1,))


def first_body(dims, kernel, profiles, adjoint, fraction, mixed_out, kron_out, up, down, west, east, *rest):
    low, mix, mixed, kron, mixed_sem, kron_sem = rest
    tracers, levels, rows = dims
    kron[...] = expand_kernel(kernel[...], levels, low.shape[0] // rows, rows)
    kron_copy = pltpu.make_async_copy(kron, kron_out, kron_sem)
    kron_copy.start()

    def body(k2, ks):
        detrains = [profiles[1, k].astype(F32) for k in ks]
        for t in range(tracers):
            parts = [
                d * adjoint[pl.ds(aligned((t * levels + k) * rows, rows), rows), :] for d, k in zip(detrains, ks)
            ]
            store_low(low, k2, rows, t, parts if len(parts) == 2 else parts + [jnp.zeros_like(parts[0])])

    over_levels(levels, body)
    convect(dims, adjoint, low, mix, kron, profiles, mixed)
    mixed_copy = pltpu.make_async_copy(mixed, mixed_out, mixed_sem)
    mixed_copy.start()
    send_edges(dims, mixed, up, down, west, east)
    count = tracers * levels
    lat = lax.axis_index("lat")
    last = lax.axis_size("lat") - 1
    f = [fraction[0, d, 0].astype(F32) for d in range(4)]
    pad = jnp.zeros((up.shape[0] - count - 1, LANES), F32)
    up[count:, :] = jnp.concatenate([jnp.where(lat < last, f[2][rows - 1 :], 0.0), pad], axis=0).astype(BF16)
    down[count:, :] = jnp.concatenate([jnp.where(lat > 0, f[3][:1], 0.0), pad], axis=0).astype(BF16)
    at = (count * rows + LANES - 1) // LANES * LANES
    west[:, at : at + tracers * rows] = end_columns(jnp.concatenate([f[1]] * tracers, axis=0))[0:1]
    east[:, at : at + tracers * rows] = end_columns(jnp.concatenate([f[0]] * tracers, axis=0))[1:2]
    kron_copy.wait()
    mixed_copy.wait()


def unpack_halo(dims, north, south, east, west, north_scr, south_scr, sides):
    tracers, levels, rows = dims
    count = tracers * levels
    north_scr[0:count, :] = north[0:count, :].astype(F32)
    south_scr[0:count, :] = south[0:count, :].astype(F32)
    sides[...] = spread_columns(west[:, 0 : count * rows], east[:, 0 : count * rows])


def transport(dims, k, fraction, mixed, north_scr, south_scr, sides):
    tracers, levels, rows = dims
    f = [fraction[0, d, k].astype(F32) for d in range(4)]
    remain = 1.0 - f[0] - f[1] - f[2] - f[3]
    lane = iota((rows, LANES), 1)
    sub = iota((rows, LANES), 0)
    out = []
    for t in range(tracers):
        index = t * levels + k
        at = pl.ds(aligned(index * rows, rows), rows)
        m = mixed[at, :]
        side = sides[at, :]
        east = jnp.where(lane == LANES - 1, side, pltpu.roll(m, LANES - 1, 1))
        west = jnp.where(lane == 0, side, pltpu.roll(m, 1, 1))
        north = jnp.where(
            sub == rows - 1,
            jnp.broadcast_to(north_scr[pl.ds(index, 1), :], (rows, LANES)),
            pltpu.roll(m, rows - 1, 0),
        )
        south = jnp.where(
            sub == 0, jnp.broadcast_to(south_scr[pl.ds(index, 1), :], (rows, LANES)), pltpu.roll(m, 1, 0)
        )
        out.append((at, remain * m + f[0] * east + f[1] * west + f[2] * north + f[3] * south))
    return out


def step_body(dims, opening, last, mixed, north, south, east, west, fraction, profiles, kron, *rest):
    surface = None
    if not opening:
        surface, *rest = rest
    if last:
        extra, rest = rest[:6], rest[6:]
    new_mixed, up, down, to_west, to_east, new_surface, north_scr, south_scr, sides, adj, low, mix = rest
    tracers, levels, rows = dims
    unpack_halo(dims, north, south, east, west, north_scr, south_scr, sides)

    def body(k2, ks):
        parts = [[] for _ in range(tracers)]
        for k in ks:
            detrain = profiles[1, k].astype(F32)
            for t, (at, value) in enumerate(transport(dims, k, fraction, mixed, north_scr, south_scr, sides)):
                adj[at, :] = value
                parts[t].append(detrain * value)
        for t in range(tracers):
            two = parts[t] if len(ks) == 2 else parts[t] + [jnp.zeros_like(parts[t][0])]
            store_low(low, k2, rows, t, two)

    over_levels(levels, body)
    convect(dims, adj, low, mix, kron, profiles, new_mixed)
    send_edges(dims, new_mixed, up, down, to_west, to_east)
    total = [adj[t * levels * rows : t * levels * rows + rows, :] for t in range(tracers)]
    if surface is not None:
        total = [surface[t * rows : (t + 1) * rows, :] + total[t] for t in range(tracers)]
    if last:
        patch(dims, new_mixed, total, *extra, new_surface)
        at = up.shape[0] - new_surface.shape[0]
        up[at:, :] = new_surface[...]
        down[at:, :] = new_surface[...]
    else:
        new_surface[...] = jnp.concatenate(total, axis=0)


def patch(dims, mixed, total, fraction, forcing, north, south, east, west, out):
    tracers, levels, rows = dims
    count = tracers * levels
    f = [fraction[0, d, 0].astype(F32) for d in range(4)]
    remain = 1.0 - f[0] - f[1] - f[2] - f[3]
    lane = iota((rows, LANES), 1)
    sub = iota((rows, LANES), 0)
    below = south[count : count + 8, :].astype(F32)[0:1]
    above = north[count : count + 8, :].astype(F32)[0:1]
    tile, under, over = [], [], []
    for t in range(tracers):
        m = mixed[t * levels * rows : t * levels * rows + rows, :]
        value = remain * m
        value = value + f[0] * jnp.where(lane == LANES - 1, 0.0, pltpu.roll(m, LANES - 1, 1))
        value = value + f[1] * jnp.where(lane == 0, 0.0, pltpu.roll(m, 1, 1))
        value = value + f[2] * jnp.where(sub == rows - 1, 0.0, pltpu.roll(m, rows - 1, 0))
        value = value + f[3] * jnp.where(sub == 0, 0.0, pltpu.roll(m, 1, 0))
        tile.append(total[t] + value + forcing[0:rows, t * LANES : (t + 1) * LANES])
        under.append(below * m[0:1])
        over.append(above * m[rows - 1 : rows])
    tops = jnp.concatenate([mixed[t * levels * rows : t * levels * rows + rows, :] for t in range(tracers)], axis=0)
    columns = end_columns(tops)
    at = (count * rows + LANES - 1) // LANES * LANES
    size = tracers * rows
    to_west = columns[0:1] * west[:, at : at + size]
    to_east = columns[1:2] * east[:, at : at + size]
    ends = jnp.concatenate([to_west, to_east, jnp.zeros((6, size), F32)], axis=0)
    ends = jnp.concatenate([ends, jnp.zeros((8, LANES - size), F32)], axis=1)
    short = (-2 * tracers) % 8
    filler = [jnp.zeros((short, LANES), F32)] if short else []
    whole = jnp.concatenate(tile + under + over + filler + [ends], axis=0)
    out[...] = whole.astype(BF16)


def last_body(dims, mixed, north, south, east, west, fraction, forcing, *rest):
    adjoint, north_scr, south_scr, sides = rest
    _, levels, rows = dims
    unpack_halo(dims, north, south, east, west, north_scr, south_scr, sides)

    def body(k2, ks):
        for k in ks:
            start = aligned(k * rows, rows)
            for t, (at, value) in enumerate(transport(dims, k, fraction, mixed, north_scr, south_scr, sides)):
                adjoint[at, :] = value + forcing[pl.ds(start, rows), t * LANES : (t + 1) * LANES]

    over_levels(levels, body)


def pack_body(sizes, owner, count, cols, weights, resid, out):
    _, blocks, slots, levels, tracers, chunk = sizes
    own = owner[...].astype(F32)
    wide = jnp.broadcast_to(own, (blocks, blocks))
    below = iota((blocks, blocks), 0)
    along = iota((blocks, blocks), 1)
    own_col = jnp.sum(jnp.where(below == along, wide, 0.0), axis=1, keepdims=True)
    earlier = jnp.where((own_col == wide) & (below < along), 1.0, 0.0)
    rank = jnp.sum(earlier, axis=0, keepdims=True)
    table = jnp.concatenate(
        [own, rank, count[...].astype(F32), jnp.zeros((5, blocks), F32)], axis=0
    ).astype(BF16)
    total = blocks * slots
    spread = (iota((blocks, total), 1) // slots == iota((blocks, total), 0)).astype(BF16)
    each = jnp.dot(table, spread, preferred_element_type=F32)
    slot = iota((1, total), 1) % slots
    target = (each[0:1].astype(jnp.int32) * CAPACITY + each[1:2].astype(jnp.int32)) * slots + slot
    valid = slot < each[2:3].astype(jnp.int32)
    held = jnp.where(valid, resid[...].astype(F32), 0.0)
    place = cols[...]
    high = (place // LANES).astype(F32)
    lower = (place % LANES).astype(F32)
    fill = LANES - levels - tracers - 2
    data = jnp.concatenate(
        [weights[...].astype(F32), held, high, lower, jnp.zeros((fill, total), F32)], axis=0
    ).astype(BF16)

    def body(c, carry):
        at = aligned(c * chunk, chunk)
        pick = jnp.where(iota((chunk, total), 0) + at == target, 1.0, 0.0).astype(BF16)
        out[pl.ds(at, chunk), :] = dot_nt(pick, data).astype(BF16)
        return carry

    lax.fori_loop(0, out.shape[0] // chunk, body, 0)


def forcing_body(dims, chunk, got, forcing, left, right):
    tracers, levels, rows = dims
    padded = left.shape[0] // rows

    def body(c, carry):
        at = aligned(c * chunk, chunk)
        part = got[pl.ds(at, chunk), :].astype(F32)
        lane = iota((chunk, LANES), 1).astype(F32)
        hit = part[:, levels + tracers + 1 : levels + tracers + 2] == lane
        for t in range(tracers):
            right[:, t * LANES : (t + 1) * LANES] = jnp.where(
                hit, part[:, levels + t : levels + t + 1], 0.0
            ).astype(BF16)
        turned = part.T
        high = turned[levels + tracers : levels + tracers + 1, :]
        sub = iota((rows, chunk), 0).astype(F32)
        mine = sub == high
        for k2 in range(padded // 2):
            two = []
            for k in (2 * k2, 2 * k2 + 1):
                two.append(jnp.where(mine, turned[k : k + 1, :], 0.0) if k < levels else jnp.zeros((rows, chunk), F32))
            left[2 * k2 * rows : (2 * k2 + 2) * rows, :] = jnp.concatenate(two, axis=0).astype(BF16)
        value = jnp.dot(left[...], right[...], preferred_element_type=F32)

        @pl.when(c == 0)
        def _():
            forcing[...] = value

        @pl.when(c > 0)
        def _():
            forcing[...] += value

        return carry

    lax.fori_loop(0, got.shape[0] // chunk, body, 0)


def lat_body(tracers, rows, offsets, matrix, *rest):
    *parts, out = rest
    size = tracers * rows
    total_rows = matrix.shape[0]
    bands = total_rows // rows
    lat = lax.axis_index("lat")
    depth = size + (2 * tracers + 7) // 8 * 8
    each = depth + 8
    width = each * len(parts)
    own = matrix[pl.ds(pl.multiple_of(lat * rows, rows), rows), :]
    own = jnp.concatenate([own] * tracers, axis=0)
    column = iota((1, width), 1) % each
    band = jnp.zeros((1, width), jnp.int32)
    for b, offset in enumerate(offsets):
        band = jnp.where(iota((1, width), 1) // each == b, lax.rem(lat + offset + bands, bands), band)
    in_band = jnp.where(column < size, column % rows, jnp.where(column < size + tracers, -1, rows))
    source = jnp.where(column < size + 2 * tracers, band * rows + in_band, -1)
    of_tracer = jnp.where(column < size, column // rows, (column - size) % tracers)
    hit = (iota((total_rows, width), 0) == source).astype(BF16)
    same = iota((size, width), 0) // rows == of_tracer
    weights = jnp.where(same, jnp.dot(own, hit, preferred_element_type=F32), 0.0).astype(BF16)
    patches = jnp.concatenate([p[p.shape[0] - each :, :] for p in parts], axis=0)
    total = jnp.dot(weights, patches, preferred_element_type=F32)
    ends = jnp.concatenate([p[p.shape[0] - 8 :, 0:each].astype(F32) for p in parts], axis=1).astype(BF16)
    ends = dot_nt(ends, weights)
    ends = jnp.concatenate([ends, jnp.zeros((8, LANES - size), F32)], axis=1)
    out[...] = jnp.concatenate([total, ends], axis=0)


def pair_body(own, other, out):
    half = own.shape[0]
    first_core = lax.axis_index("lon") % 2 == 0
    out[0:half, :] = jnp.where(first_core, own[...], other[...])
    out[half:, :] = jnp.where(first_core, other[...], own[...])


def lon_body(matrix, *rest):
    *pairs, out = rest
    half = pairs[0].shape[0] // 2
    parts = [p[at : at + half, :] for p in pairs for at in (half, 0)]
    count = len(parts)
    size = out.shape[0]
    lon = lax.axis_index("lon") // 2 * 2 + 1
    ends = [p[size : size + 8, :].astype(F32)[:, 0:size] for p in parts]
    east = jnp.concatenate([ends[(s + 1) % count][1:2] for s in range(count)], axis=1)
    west = jnp.concatenate([ends[(s - 1) % count][0:1] for s in range(count)], axis=1)
    sides = spread_columns(east, west)
    blocks, owns = [], []
    for s, part in enumerate(parts):
        blocks.append((part[0:size, :].astype(F32) + sides[s * size : (s + 1) * size, :]).astype(BF16))
        source = lax.rem(lon - s + count, count)
        owns.append(matrix[:, pl.ds(pl.multiple_of(source * LANES, LANES), LANES)])
    out[...] = dot_nt(jnp.concatenate(blocks, axis=1), jnp.concatenate(owns, axis=1))


def ring(axis, step):
    count = lax.axis_size(axis)
    return [(i, (i + step) % count) for i in range(count)]


def exchange(up, down, to_west, to_east):
    south = lax.ppermute(up, "lat", ring("lat", 1))
    north = lax.ppermute(down, "lat", ring("lat", -1))
    east = lax.ppermute(to_west, "lon", ring("lon", -1))
    west = lax.ppermute(to_east, "lon", ring("lon", 1))
    return north, south, east, west


def window(
    adjoint_in,
    fractions,
    profiles,
    kernel,
    obs_weights,
    obs_resid,
    obs_cols,
    obs_owner,
    obs_count,
    lat_matrix,
    lon_matrix,
):
    dims = tracers, levels, rows = adjoint_in.shape[:3]
    assert adjoint_in.shape[3] == LANES
    padded = (levels + 1) // 2 * 2
    count = tracers * levels
    cells = count * rows
    wide = tracers * LANES
    devices = lax.axis_size(BOTH)
    state = jax.ShapeDtypeStruct((cells, LANES), F32)
    row_edge = jax.ShapeDtypeStruct((count, LANES), BF16)
    side_edge = jax.ShapeDtypeStruct((1, cells), F32)
    edges = [row_edge, row_edge, side_edge, side_edge]
    long_row = jax.ShapeDtypeStruct((count + 16, LANES), BF16)
    long_side = jax.ShapeDtypeStruct((1, (cells + LANES - 1) // LANES * LANES + LANES), F32)
    long_edges = [long_row, long_row, long_side, long_side]
    level_zero = pl.BlockSpec((1, 4, 1, rows, LANES), lambda i: (0, 0, 0, 0, 0))
    kron_type = jax.ShapeDtypeStruct((padded * rows, padded * rows), BF16)
    surface_type = jax.ShapeDtypeStruct((tracers * rows, LANES), F32)
    low_scr = pltpu.VMEM((padded * rows, wide), BF16)
    mix_scr = pltpu.VMEM((padded * rows, wide), F32)
    halo_scr = [
        pltpu.VMEM(((count + 7) // 8 * 8, LANES), F32),
        pltpu.VMEM(((count + 7) // 8 * 8, LANES), F32),
        pltpu.VMEM((cells, LANES), F32),
    ]

    def spec(leaf):
        return full(leaf.shape)

    mixed, kron, *out = pl.pallas_call(
        functools.partial(first_body, dims),
        grid=(1,),
        out_shape=[state, kron_type] + long_edges,
        in_specs=[full(kernel.shape), full(profiles.shape), spec(state), level_zero],
        out_specs=[pl.BlockSpec(memory_space=pltpu.HBM)] * 2 + [spec(s) for s in long_edges],
        scratch_shapes=[
            low_scr,
            mix_scr,
            pltpu.VMEM(state.shape, state.dtype),
            pltpu.VMEM(kron_type.shape, kron_type.dtype),
            pltpu.SemaphoreType.DMA,
            pltpu.SemaphoreType.DMA,
        ],
        compiler_params=params(60 << 20),
        name="first",
    )(kernel, profiles, adjoint_in.reshape(cells, LANES), fractions)
    halo = first_halo = exchange(*out)
    obs_count, _ = lax.optimization_barrier((obs_count, out[2]))

    blocks = obs_count.shape[0]
    slots = obs_cols.shape[0] // blocks
    rows_out = devices * CAPACITY * slots
    packed = pl.pallas_call(
        functools.partial(pack_body, (devices, blocks, slots, levels, tracers, 8 * CAPACITY * slots)),
        grid=(1,),
        out_shape=jax.ShapeDtypeStruct((rows_out, LANES), BF16),
        in_specs=[
            full((1, blocks)),
            full((1, blocks)),
            full((1, blocks * slots)),
            full(obs_weights.shape),
            full(obs_resid.shape),
        ],
        out_specs=full((rows_out, LANES)),
        compiler_params=params(),
        name="pack",
    )(
        obs_owner.reshape(1, blocks),
        obs_count.reshape(1, blocks),
        obs_cols.reshape(1, blocks * slots),
        obs_weights,
        obs_resid,
    )
    got = lax.all_to_all(
        packed.reshape(devices, CAPACITY * slots, LANES), BOTH, split_axis=0, concat_axis=0, tiled=True
    )
    chunk = min(rows_out, 1536)
    forcing = pl.pallas_call(
        functools.partial(forcing_body, dims, chunk),
        out_shape=jax.ShapeDtypeStruct((padded * rows, wide), F32),
        scratch_shapes=[pltpu.VMEM((padded * rows, chunk), BF16), pltpu.VMEM((chunk, wide), BF16)],
        compiler_params=params(),
        name="forcing",
    )(got.reshape(rows_out, LANES))

    lon_count = lax.axis_size("lon")
    patch_rows = (tracers * (rows + 2) + 7) // 8 * 8
    patch_type = jax.ShapeDtypeStruct((patch_rows + 8, LANES), BF16)
    tall = jax.ShapeDtypeStruct(((count + 15) // 16 * 16 + patch_type.shape[0], LANES), BF16)
    for step_index in range(STEPS - 1, 0, -1):
        last = step_index == 1
        frac_spec = pl.BlockSpec((1,) + fractions.shape[1:], lambda i, n=step_index: (n, 0, 0, 0, 0))
        halo_types = long_edges if step_index == STEPS - 1 else edges
        outs = [tall, tall, side_edge, side_edge] if last else edges
        opening = step_index == STEPS - 1
        ins = [mixed, *halo, fractions, profiles, kron]
        in_specs = [spec(state)] + [spec(h) for h in halo_types]
        in_specs += [frac_spec, full(profiles.shape), spec(kron_type)]
        if not opening:
            ins.append(surface)
            in_specs.append(spec(surface_type))
        result = surface_type
        if last:
            ins += [fractions, forcing, *first_halo]
            in_specs += [level_zero, pl.BlockSpec((rows, wide), lambda i: (0, 0))] + [spec(h) for h in long_edges]
            result = patch_type
        mixed, *out, surface = pl.pallas_call(
            functools.partial(step_body, dims, opening, last),
            grid=(1,),
            out_shape=[state] + outs + [result],
            in_specs=in_specs,
            out_specs=[spec(s) for s in [state] + outs + [result]],
            scratch_shapes=halo_scr + [pltpu.VMEM((cells, LANES), F32), low_scr, mix_scr],
            compiler_params=params(),
            name="step",
        )(*ins)
        halo = exchange(*out)

    lat_count = lax.axis_size("lat")
    parts = [surface, halo[1], halo[0]]
    offsets = [0, -1, 1]
    for shift in range(2, lat_count - 1):
        parts.append(lax.ppermute(surface, "lat", ring("lat", shift)))
        offsets.append(-shift)
    bands = pl.pallas_call(
        functools.partial(lat_body, tracers, rows, offsets),
        out_shape=jax.ShapeDtypeStruct((tracers * rows + 8, LANES), F32),
        compiler_params=params(),
        name="lat_smooth",
    )(lat_matrix, *parts)
    other = lax.ppermute(bands, "lon", [(i, i ^ 1) for i in range(lon_count)])
    pair = pl.pallas_call(
        pair_body,
        out_shape=jax.ShapeDtypeStruct((2 * bands.shape[0], LANES), F32),
        compiler_params=params(),
        name="pair",
    )(bands, other)
    shifts = [lax.ppermute(pair, "lon", ring("lon", shift)) for shift in range(2, lon_count, 2)]
    frac_spec = pl.BlockSpec((1,) + fractions.shape[1:], lambda i: (0, 0, 0, 0, 0))
    adjoint = pl.pallas_call(
        functools.partial(last_body, dims),
        grid=(1,),
        out_shape=state,
        in_specs=[spec(state), spec(tall), spec(tall), spec(side_edge), spec(side_edge)]
        + [frac_spec, full(forcing.shape)],
        out_specs=spec(state),
        scratch_shapes=halo_scr,
        compiler_params=params(),
        name="last",
    )(mixed, *halo, fractions, forcing)
    smoothed = pl.pallas_call(
        lon_body,
        out_shape=surface_type,
        compiler_params=params(),
        name="lon_smooth",
    )(lon_matrix, pair, *shifts)
    return adjoint.reshape(adjoint_in.shape), smoothed.reshape(tracers, rows, LANES)


def solution(mesh):
    placed = (
        P(None, None, "lat", "lon"),
        P(None, None, None, "lat", "lon"),
        P(None, None, "lat", "lon"),
        P(),
        P(None, BOTH),
        P(None, BOTH),
        P(BOTH),
        P(BOTH, None),
        P(BOTH),
        P(),
        P("lon", None),
    )
    return jax.shard_map(
        window,
        mesh=mesh,
        in_specs=placed,
        out_specs=(P(None, None, "lat", "lon"), P(None, "lat", "lon")),
        check_vma=False,
    )
```
